768 devices in a mesh: ct: 16 (over z_hi, y), tile: 48 (over x, z_lo, core).
Axes of the slice: x: 4, y: 8, z: 12 (z_hi: 2, z_lo: 6; z = z_hi * 6 + z_lo), core: 2. Of those that a mesh axis runs over, the one named last changes fastest.
Arguments:
- voltages: int32 [48, 256, 2048], P('tile', 'ct'), may hold values from -8 to 7
- fir_taps: float32 [4, 1024], replicated, may hold values from -3 to 3
- tile_map: int32 [528, 2], P('tile'), may hold values from 0 to 31, as said below
Outputs:
- visibilities: float32 [528, 1024, 128], P('tile', 'ct')
The draws below stay inside these ranges and needn't reach their ends.
Inputs may be any that keep to these rules, and one draw needn't show every extreme that they name: `tile_map`: each row holds two block numbers, the first not above the second; every such pair of the 32 blocks stands in exactly one row.
All inputs are finite; a program needn't handle non-finite values.
Results may differ from the reference program's by a relative error of at most 0.0056.
Values may be sent and summed in bfloat16 or wider, within the bound.
No kernel may reach another device: no remote copies, remote signals or barrier semaphores. Data moves between devices by JAX's collectives and lax.ppermute only.
A program may use at most 32 MiB of HBM per device.

```python
import math
import jax
import jax.numpy as jnp
import numpy as np
from jax import lax

NCHAN = 1024
INPUTS = 256
TAPS = 4
B = 8
TIME = 48
NB = 32
TILES = 528


def draw_tile_map(key, part):
    block_pairs = np.array([(first, second) for first in range(NB) for second in range(first, NB)], dtype=np.int32)
    shuffled = jax.random.permutation(key, TILES)
    return jnp.asarray(block_pairs)[shuffled]


def plant(values, rng, least, high):
    longest = values.shape.index(max(values.shape))
    spots = []
    for shift in (0, 1):
        where = [jax.random.randint(jax.random.fold_in(rng, axis), (), 0, length) for axis, length in enumerate(values.shape)]
        where[longest] = (where[longest] + shift) % values.shape[longest]
        spots.append(tuple(where))
    return values.at[spots[0]].set(least).at[spots[1]].set(high)


def noise(rng, shape, scale, limit, kind=jnp.bfloat16):
    values = jax.random.normal(rng, shape, jnp.float32) * scale
    return jnp.minimum(jnp.maximum(values, -limit), limit).astype(kind)


def setup_inputs(seed: int = 0) -> dict:
    keys = jax.random.split(jax.random.key(seed), 4)
    return {
        "voltages": plant(jax.random.randint(keys[0], (TIME, INPUTS, 2 * NCHAN), -8, 8), jax.random.fold_in(keys[0], 1), -8, 7).astype(jnp.int32),
        "fir_taps": noise(keys[1], (TAPS, NCHAN), TAPS ** -0.5, 3.0, jnp.float32),
        "tile_map": draw_tile_map(jax.random.fold_in(keys[3], 71), 0),
    }


def dft_table(channels):
    positions = jnp.arange(channels, dtype=jnp.int32)
    products = positions[:, None] * positions[None, :] % channels
    angles = products.astype(jnp.float32) * (2.0 * math.pi / channels)
    norm_scale = 1.0 / math.sqrt(channels)
    cosine = jnp.cos(angles) * norm_scale
    sine = jnp.sin(angles) * norm_scale
    upper_half = jnp.concatenate([cosine, -sine], axis=1)
    lower_half = jnp.concatenate([sine, cosine], axis=1)
    return jnp.concatenate([upper_half, lower_half], axis=0).astype(jnp.bfloat16)

def reference(voltages, fir_taps, tile_map):
    samples = voltages.astype(jnp.float32) * 0.25
    tap_gains = jnp.concatenate([fir_taps, fir_taps], axis=1)
    filtered = jnp.zeros(samples.shape, jnp.float32)
    for tap_index in range(TAPS):
        delayed = jnp.pad(samples[:TIME - tap_index], ((tap_index, 0), (0, 0), (0, 0)))
        filtered = filtered + tap_gains[tap_index][None, None, :] * delayed
    filtered = filtered.astype(jnp.bfloat16)
    spectra = jnp.dot(filtered.reshape(TIME * INPUTS, 2 * NCHAN), dft_table(NCHAN), preferred_element_type=jnp.float32).astype(jnp.bfloat16)
    blocks = spectra.reshape(TIME, NB, B, 2, NCHAN).astype(jnp.float32)

    def one_tile(block_pair):
        left_side = lax.dynamic_index_in_dim(blocks, block_pair[0], axis=1, keepdims=False)
        right_side = lax.dynamic_index_in_dim(blocks, block_pair[1], axis=1, keepdims=False)
        swapped = jnp.stack([left_side[:, :, 1], -left_side[:, :, 0]], axis=2)
        stacked = jnp.stack([left_side, swapped], axis=0)
        sums = jnp.einsum('qtapc,tbpc->cqab', stacked, right_side, precision=lax.Precision.HIGHEST)
        return sums.reshape(NCHAN, 2 * B * B) / TIME
    return lax.map(one_tile, tile_map)
```

```python
import math

import jax
import jax.numpy as jnp
import ml_dtypes
import numpy as np
from jax import lax
from jax.experimental import pallas as pl
from jax.experimental.pallas import tpu as pltpu
from jax.sharding import Mesh, PartitionSpec as P

NCHAN = 1024
TIME = 48
LANES = 128
ZH, Y, X, ZQ, ZR, C = 2, 8, 4, 3, 2, 2
TILE_AXES = ("x", "zq", "zr", "c")
OWN = 11
VMEM = 48 * 1024 * 1024

BF = jnp.bfloat16
F32 = jnp.float32


def dft_tables():
    y, x, zh, zr, c = np.meshgrid(*(np.arange(n) for n in (Y, X, ZH, ZR, C)), indexing="ij")
    first = ((zh * Y + y) * 64 + ((x * ZR + zr) * C + c) * 4).reshape(-1)
    channels = first[None, :] + np.arange(4)[:, None]
    products = channels[:, :, None] * np.arange(NCHAN)[None, None, :] % NCHAN
    angles = products.astype(np.float32) * np.float32(2.0 * math.pi / NCHAN)
    scale = np.float32(1.0 / math.sqrt(NCHAN))
    return tuple((f(angles) * scale).astype(ml_dtypes.bfloat16) for f in (np.cos, np.sin))


def swap_chunks(rows, width):
    rows = list(rows)
    chunk = lax.broadcasted_iota(jnp.int32, rows[0].shape, 1) // width
    step = len(rows) // 2
    while step:
        low = (chunk & step) == 0
        for g in range(len(rows)):
            if not g & step:
                a, b = rows[g], rows[g + step]
                rows[g] = jnp.where(low, a, pltpu.roll(b, step * width, 1))
                rows[g + step] = jnp.where(low, pltpu.roll(a, LANES - step * width, 1), b)
        step //= 2
    return rows


def dot(a, b, contract):
    return lax.dot_general(a, b, ((contract[:1], contract[1:]), ((), ())), preferred_element_type=F32)


def filter_kernel(map_ref, v0_ref, v1_ref, v2_ref, v3_ref, fir_ref, cos_ref, sin_ref, out_ref, w_ref, acc_ref):
    step = pl.program_id(0)

    @pl.when(step == 0)
    def _():
        halves = []
        for p in range(2):
            total = None
            for k, ref in enumerate((v0_ref, v1_ref, v2_ref, v3_ref)):
                part = ref[:, p * NCHAN : (p + 1) * NCHAN].astype(F32) * 0.25
                term = fir_ref[k : k + 1, :] * part
                total = term if total is None else total + term
            halves.append(total.astype(BF).astype(F32))
        re, im = halves
        w_ref[0] = jnp.concatenate([re, im] * 4, axis=0).astype(BF)
        w_ref[1] = jnp.concatenate([im, -re] * 4, axis=0).astype(BF)
        acc_ref[...] = jnp.zeros_like(acc_ref)

    block = lax.broadcasted_iota(jnp.int32, (LANES, NCHAN), 0) // 32
    here = block == step
    total = acc_ref[...]
    for i, ref in enumerate((cos_ref, sin_ref)):
        weights = jnp.where(here, w_ref[i].astype(F32), 0.0).astype(BF)
        total = total + dot(ref[0], weights, (1, 1))
    acc_ref[...] = total

    @pl.when(step == pl.num_programs(0) - 1)
    def _():
        own = (lax.axis_index("x") * ZR + lax.axis_index("zr")) * C + lax.axis_index("c")
        sub = lax.broadcasted_iota(jnp.int32, (8, LANES), 0)
        place = lax.broadcasted_iota(jnp.int32, (8, LANES), 1) + (sub % 2) * LANES - own * 16
        tiles = jnp.zeros((8, LANES), jnp.int32)
        for l in range(OWN):
            tiles = jnp.where(place == l, jnp.where(sub < 2, map_ref[0, l], map_ref[1, l]), tiles)
        tiles = jnp.where(sub < 4, tiles, 0).astype(F32)
        data = acc_ref[...].reshape(Y * X, 8, LANES)
        both = jnp.concatenate([data, jnp.broadcast_to(tiles[None], data.shape)], axis=1)
        out_ref[...] = both.astype(BF)


def turn_kernel(in_ref, out_ref, f_ref):
    f_ref[...] = in_ref[...].astype(F32).reshape(f_ref.shape)
    tiles = sum(f_ref[x * 16 + 8 : x * 16 + 16, :] for x in range(X))
    for zh in range(ZH):
        for z in range(ZR * C):
            d = zh * ZR * C + z
            rows = [f_ref[pl.ds(x * 16 + d, Y, stride=64), :] for x in range(X)]
            block = jnp.concatenate(rows + [tiles], axis=0).astype(BF)
            for zq in range(ZQ):
                out_ref[(zh * ZQ + zq) * ZR * C + z] = block


def correlate_kernel(in_ref, out_ref, f_ref, a_ref, c_ref, d_ref):
    f_ref[: 24 * 40] = in_ref[...].astype(F32).reshape(24 * 40, LANES)
    f_ref[24 * 40 :] = jnp.zeros((64, LANES), F32)
    row = lax.broadcasted_iota(jnp.int32, (64, LANES), 0)
    frame = (row % 5 != 4) & (row < 60)
    for zh in range(ZH):
        groups = [jnp.where(frame, f_ref[pl.ds(zh * 480 + y, 64, stride=8), :], 0.0) for y in range(Y)]
        for k, part in enumerate(swap_chunks(groups, 16)):
            ch, p = divmod(k, 2)
            a_ref[ch, p * 64 : (p + 1) * 64, zh * LANES : (zh + 1) * LANES] = part.astype(BF)

    i = lax.broadcasted_iota(jnp.int32, (256, 256), 0)
    j = lax.broadcasted_iota(jnp.int32, (256, 256), 1)
    order = jnp.where(i == (j % 32) * 8 + j // 32, 1.0, 0.0).astype(BF)
    for ch in range(4):
        cols = a_ref[ch]
        left = dot(cols, order, (1, 0))
        re, im = left[:64], left[64:]
        both = jnp.concatenate([jnp.concatenate([re, im], axis=0), jnp.concatenate([im, -re], axis=0)], axis=1)
        c_ref[...] = dot(both.astype(BF), cols, (0, 0)) * (1.0 / TIME)
        for block, (h, g) in enumerate(((0, 0), (1, 0), (1, 1))):
            rows = [c_ref[k * 32 + g * 16 : k * 32 + g * 16 + 16, h * LANES : (h + 1) * LANES] for k in range(16)]
            for s, part in enumerate(swap_chunks(rows, 8)):
                at = block * 256 + s * 16
                d_ref[at : at + 16, ch * LANES : (ch + 1) * LANES] = part.astype(BF)

    first = lax.axis_index("zq") * 160 + 32
    tiles = sum(f_ref[pl.ds(pl.multiple_of(first + 40 * k, 8), 8), :] for k in range(ZR * C))
    r = jnp.concatenate([tiles[0:1], tiles[1:2]], axis=1).astype(jnp.int32)
    s = jnp.concatenate([tiles[2:3], tiles[3:4]], axis=1).astype(jnp.int32)
    rh, sh = jnp.where(r >= 16, 1, 0), jnp.where(s >= 16, 1, 0)
    index = (rh + sh) * 256 + (s - 16 * sh) * 16 + (r - 16 * rh)
    pick = jnp.where(lax.broadcasted_iota(jnp.int32, (768, 256), 0) == index, 1.0, 0.0).astype(BF)
    picked = dot(pick, d_ref[...], (0, 0)).astype(BF)
    for d in range(16):
        for ch in range(4):
            out_ref[d, ch * 16 : (ch + 1) * 16, :] = picked[d * 16 : (d + 1) * 16, ch * LANES : (ch + 1) * LANES]


def place_kernel(in_ref, out_ref, f_ref):
    f_ref[...] = in_ref[...].astype(F32).reshape(f_ref.shape)
    for l in range(OWN):
        out_ref[l] = f_ref[pl.ds(l, 64, stride=16), :]


PARAMS = pltpu.CompilerParams(vmem_limit_bytes=VMEM)


def per_device(voltages, fir_taps, tile_map):
    own = voltages[0].astype(BF)
    count = X * ZQ * ZR * C
    before = [lax.ppermute(own, TILE_AXES, [(t, t + k) for t in range(count - k)]) for k in (1, 2, 3)]
    cos, sin = dft_tables()
    whole = lambda *shape: pl.BlockSpec(shape, lambda j: (0,) * len(shape))
    table = pl.BlockSpec((1, 256, NCHAN), lambda j: (j, 0, 0))
    sent = pl.pallas_call(
        filter_kernel,
        out_shape=jax.ShapeDtypeStruct((Y * X, 16, LANES), BF),
        grid=(4,),
        in_specs=[pl.BlockSpec(memory_space=pltpu.SMEM)]
        + [whole(16, 2 * NCHAN)] * 4
        + [whole(4, NCHAN), table, table],
        out_specs=whole(Y * X, 16, LANES),
        scratch_shapes=[pltpu.VMEM((2, LANES, NCHAN), BF), pltpu.VMEM((256, LANES), F32)],
        compiler_params=PARAMS,
        name="filter",
    )(tile_map.T, own, *before, fir_taps, jnp.asarray(cos), jnp.asarray(sin))
    came = lax.all_to_all(sent, ("y", "x"), 0, 0, tiled=True)
    sent = pl.pallas_call(
        turn_kernel,
        out_shape=jax.ShapeDtypeStruct((ZH * ZQ * ZR * C, 40, LANES), BF),
        scratch_shapes=[pltpu.VMEM((Y * X * 16, LANES), F32)],
        compiler_params=PARAMS,
        name="turn",
    )(came)
    came = lax.all_to_all(sent, ("zh", "zq", "zr", "c"), 0, 0, tiled=True)
    sent = pl.pallas_call(
        correlate_kernel,
        out_shape=jax.ShapeDtypeStruct((16, 64, LANES), BF),
        scratch_shapes=[
            pltpu.VMEM((1024, LANES), F32),
            pltpu.VMEM((4, LANES, 256), BF),
            pltpu.VMEM((512, 256), F32),
            pltpu.VMEM((768, 512), BF),
        ],
        compiler_params=PARAMS,
        name="correlate",
    )(came)
    came = lax.all_to_all(sent, ("x", "zr", "c"), 0, 0, tiled=True)
    return pl.pallas_call(
        place_kernel,
        out_shape=jax.ShapeDtypeStruct((OWN, 64, LANES), F32),
        scratch_shapes=[pltpu.VMEM((1024, LANES), F32)],
        compiler_params=PARAMS,
        name="place",
    )(came)


def solution(mesh):
    fine = Mesh(mesh.devices.reshape(ZH, Y, X, ZQ, ZR, C), ("zh", "y") + TILE_AXES)
    in_specs = (P(TILE_AXES, ("zh", "y"), None), P(), P(TILE_AXES, None))
    out_specs = P(TILE_AXES, ("zh", "y"), None)
    return jax.shard_map(per_device, mesh=fine, in_specs=in_specs, out_specs=out_specs, check_vma=False)
```

```python
import math

import jax
import jax.numpy as jnp
import ml_dtypes
import numpy as np
from jax import lax
from jax.experimental import pallas as pl
from jax.experimental.pallas import tpu as pltpu
from jax.sharding import Mesh, PartitionSpec as P

NCHAN = 1024
QUARTER = NCHAN // 4
TIME = 48
LANES = 128
ZH, Y, X, ZQ, ZR, C = 2, 8, 4, 3, 2, 2
TILE_AXES = ("x", "zq", "zr", "c")
OWN = 11
SLOT = 12
VMEM = 48 * 1024 * 1024

BF = jnp.bfloat16
F32 = jnp.float32


def dft_table():
    y, x, zh, zr, c = np.meshgrid(*(np.arange(n) for n in (Y, X, ZH, ZR, C)), indexing="ij")
    first = ((zh * Y + y) * 64 + ((x * ZR + zr) * C + c) * 4).reshape(-1)
    channels = first[:, None] + np.arange(4)[None, :]
    products = channels[:, :, None] * np.arange(QUARTER)[None, None, :] % NCHAN
    angles = products.astype(np.float32) * np.float32(2.0 * math.pi / NCHAN)
    scale = np.float32(1.0 / math.sqrt(NCHAN))
    both = np.stack([np.cos(angles) * scale, np.sin(angles) * scale], axis=2)
    return both.reshape(256, 8 * QUARTER).astype(ml_dtypes.bfloat16)


def swap_chunks(rows, width):
    rows = list(rows)
    chunk = lax.broadcasted_iota(jnp.int32, rows[0].shape, 1) // width
    step = len(rows) // 2
    while step:
        low = (chunk & step) == 0
        for g in range(len(rows)):
            if not g & step:
                a, b = rows[g], rows[g + step]
                rows[g] = jnp.where(low, a, pltpu.roll(b, step * width, 1))
                rows[g + step] = jnp.where(low, pltpu.roll(a, LANES - step * width, 1), b)
        step //= 2
    return rows


def dot(a, b, contract):
    return lax.dot_general(a, b, ((contract[:1], contract[1:]), ((), ())), preferred_element_type=F32)


def prepare_kernel(map_hbm, volts_hbm, fir_hbm, table_hbm, own_ref, fir_ref, table_ref, tiles_ref, map_ref, volts_ref, sems):
    copies = [
        pltpu.make_async_copy(volts_hbm.at[0], volts_ref, sems.at[0]),
        pltpu.make_async_copy(fir_hbm, fir_ref, sems.at[1]),
        pltpu.make_async_copy(table_hbm, table_ref, sems.at[2]),
        pltpu.make_async_copy(map_hbm, map_ref, sems.at[3]),
    ]
    for copy in copies:
        copy.start()
    copies[0].wait()
    own_ref[...] = volts_ref[...].astype(F32).astype(BF)
    own = (lax.axis_index("x") * ZR + lax.axis_index("zr")) * C + lax.axis_index("c")
    copies[3].wait()
    sub = lax.broadcasted_iota(jnp.int32, (8, LANES), 0)
    place = lax.broadcasted_iota(jnp.int32, (8, LANES), 1) + (sub % 2) * LANES - own * SLOT
    tiles = jnp.zeros((8, LANES), jnp.int32)
    for l in range(OWN):
        tiles = jnp.where(place == l, jnp.where(sub < 2, map_ref[0, l], map_ref[1, l]), tiles)
    tiles_ref[...] = jnp.where(sub < 4, tiles, 0).astype(F32)
    copies[1].wait()
    copies[2].wait()


def filter_kernel(v0_ref, v1_ref, v2_ref, v3_ref, fir_ref, table_ref, tiles_ref, out_ref):
    re, im = [], []
    for p, parts in enumerate((re, im)):
        for q in range(4):
            at = q * QUARTER
            total = None
            for k, ref in enumerate((v0_ref, v1_ref, v2_ref, v3_ref)):
                part = ref[:, p * NCHAN + at : p * NCHAN + at + QUARTER].astype(F32) * 0.25
                term = fir_ref[k : k + 1, at : at + QUARTER] * part
                total = term if total is None else total + term
            parts.append(total.astype(BF).astype(F32))
    evens = [(x[0] + x[2], x[1] + x[3]) for x in (re, im)]
    odds = [(x[0] - x[2], x[1] - x[3]) for x in (re, im)]
    sums = (
        (evens[0][0] + evens[0][1], evens[1][0] + evens[1][1]),
        (odds[0][0] + odds[1][1], odds[1][0] - odds[0][1]),
        (evens[0][0] - evens[0][1], evens[1][0] - evens[1][1]),
        (odds[0][0] - odds[1][1], odds[1][0] + odds[0][1]),
    )
    total = None
    for j, (r, m) in enumerate(sums):
        live = jnp.concatenate([jnp.concatenate([r, m], axis=1), jnp.concatenate([m, -r], axis=1)], axis=0).astype(BF)
        rows = [jnp.zeros((32, 2 * QUARTER), BF)] * 4
        rows[j] = live
        part = dot(table_ref[:, j * 2 * QUARTER : (j + 1) * 2 * QUARTER], jnp.concatenate(rows, axis=0), (1, 1))
        total = part if total is None else total + part
    data = total.reshape(Y * X, 8, LANES)
    both = jnp.concatenate([data, jnp.broadcast_to(tiles_ref[...][None], data.shape)], axis=1)
    out_ref[...] = both.astype(BF)


def turn_kernel(in_ref, out_ref, f_ref):
    f_ref[...] = in_ref[...].astype(F32).reshape(f_ref.shape)
    tiles = sum(f_ref[x * 16 + 8 : x * 16 + 16, :] for x in range(X))
    for zh in range(ZH):
        for z in range(ZR * C):
            d = zh * ZR * C + z
            rows = [f_ref[pl.ds(x * 16 + d, Y, stride=64), :] for x in range(X)]
            block = jnp.concatenate(rows + [tiles], axis=0).astype(BF)
            for zq in range(ZQ):
                out_ref[(zh * ZQ + zq) * ZR * C + z] = block


def correlate_kernel(in_ref, out_ref, f_ref, a_ref, c_ref, d_ref):
    f_ref[: 24 * 40] = in_ref[...].astype(F32).reshape(24 * 40, LANES)
    f_ref[24 * 40 :] = jnp.zeros((64, LANES), F32)
    row = lax.broadcasted_iota(jnp.int32, (64, LANES), 0)
    frame = (row % 5 != 4) & (row < 60)
    for zh in range(ZH):
        groups = [jnp.where(frame, f_ref[pl.ds(zh * 480 + y, 64, stride=8), :], 0.0) for y in range(Y)]
        for k, part in enumerate(swap_chunks(groups, 16)):
            ch, p = divmod(k, 2)
            a_ref[ch, p * 64 : (p + 1) * 64, zh * LANES : (zh + 1) * LANES] = part.astype(BF)

    i = lax.broadcasted_iota(jnp.int32, (256, 256), 0)
    j = lax.broadcasted_iota(jnp.int32, (256, 256), 1)
    order = jnp.where(i == (j % 32) * 8 + j // 32, 1.0, 0.0).astype(BF)
    for ch in range(4):
        cols = a_ref[ch]
        left = dot(cols, order, (1, 0))
        re, im = left[:64], left[64:]
        both = jnp.concatenate([jnp.concatenate([re, im], axis=0), jnp.concatenate([im, -re], axis=0)], axis=1)
        c_ref[...] = dot(both.astype(BF), cols, (0, 0)) * (1.0 / TIME)
        for block, (h, g) in enumerate(((0, 0), (1, 0), (1, 1))):
            rows = [c_ref[k * 32 + g * 16 : k * 32 + g * 16 + 16, h * LANES : (h + 1) * LANES] for k in range(16)]
            for s, part in enumerate(swap_chunks(rows, 8)):
                at = block * 256 + s * 16
                d_ref[at : at + 16, ch * LANES : (ch + 1) * LANES] = part.astype(BF)

    first = lax.axis_index("zq") * 160 + 32
    tiles = sum(f_ref[pl.ds(pl.multiple_of(first + 40 * k, 8), 8), :] for k in range(ZR * C))
    r = jnp.concatenate([tiles[0:1], tiles[1:2]], axis=1).astype(jnp.int32)
    s = jnp.concatenate([tiles[2:3], tiles[3:4]], axis=1).astype(jnp.int32)
    rh, sh = jnp.where(r >= 16, 1, 0), jnp.where(s >= 16, 1, 0)
    index = (rh + sh) * 256 + (s - 16 * sh) * 16 + (r - 16 * rh)
    pick = jnp.where(lax.broadcasted_iota(jnp.int32, (768, 256), 0) == index, 1.0, 0.0).astype(BF)
    c_ref[: 16 * SLOT, :] = dot(pick, d_ref[:, :256], (0, 0))[: 16 * SLOT]
    c_ref[256 : 256 + 16 * SLOT, :] = dot(pick, d_ref[:, 256:], (0, 0))[: 16 * SLOT]
    for d in range(16):
        for ch in range(4):
            rows = c_ref[(ch // 2) * 256 + d * SLOT : (ch // 2) * 256 + (d + 1) * SLOT, (ch % 2) * LANES : (ch % 2 + 1) * LANES]
            f_ref[d * 48 + ch * SLOT : d * 48 + (ch + 1) * SLOT, :] = rows
    out_ref[...] = f_ref[: 16 * 48, :].reshape(16, 48, LANES).astype(BF)


def place_kernel(in_ref, out_ref, f_ref):
    f_ref[...] = in_ref[...].astype(F32).reshape(f_ref.shape)
    for l in range(OWN):
        out_ref[l] = f_ref[pl.ds(l, 64, stride=SLOT), :]


PARAMS = pltpu.CompilerParams(vmem_limit_bytes=VMEM)


def per_device(voltages, fir_taps, tile_map):
    hbm = pl.BlockSpec(memory_space=pltpu.MemorySpace.HBM)
    own, fir, table, tiles = pl.pallas_call(
        prepare_kernel,
        out_shape=(
            jax.ShapeDtypeStruct((16, 2 * NCHAN), BF),
            jax.ShapeDtypeStruct((4, NCHAN), F32),
            jax.ShapeDtypeStruct((256, 8 * QUARTER), BF),
            jax.ShapeDtypeStruct((8, LANES), F32),
        ),
        in_specs=[hbm] * 4,
        scratch_shapes=[pltpu.SMEM((2, OWN), jnp.int32), pltpu.VMEM((16, 2 * NCHAN), jnp.int32), pltpu.SemaphoreType.DMA((4,))],
        compiler_params=PARAMS,
        name="prepare",
    )(*(pltpu.with_memory_space_constraint(a, pltpu.MemorySpace.HBM) for a in (tile_map.T, voltages, fir_taps, jnp.asarray(dft_table()))))
    count = X * ZQ * ZR * C
    before = [lax.ppermute(own, TILE_AXES, [(t, t + k) for t in range(count - k)]) for k in (1, 2, 3)]
    sent = pl.pallas_call(
        filter_kernel,
        out_shape=jax.ShapeDtypeStruct((Y * X, 16, LANES), BF),
        compiler_params=PARAMS,
        name="filter",
    )(own, *before, fir, table, tiles)
    came = lax.all_to_all(sent, ("y", "x"), 0, 0, tiled=True)
    sent = pl.pallas_call(
        turn_kernel,
        out_shape=jax.ShapeDtypeStruct((ZH * ZQ * ZR * C, 40, LANES), BF),
        scratch_shapes=[pltpu.VMEM((Y * X * 16, LANES), F32)],
        compiler_params=PARAMS,
        name="turn",
    )(came)
    came = lax.all_to_all(sent, ("zh", "zq", "zr", "c"), 0, 0, tiled=True)
    sent = pl.pallas_call(
        correlate_kernel,
        out_shape=jax.ShapeDtypeStruct((16, 4 * SLOT, LANES), BF),
        scratch_shapes=[
            pltpu.VMEM((1024, LANES), F32),
            pltpu.VMEM((4, LANES, 256), BF),
            pltpu.VMEM((512, 256), F32),
            pltpu.VMEM((768, 512), BF),
        ],
        compiler_params=PARAMS,
        name="correlate",
    )(came)
    came = lax.all_to_all(sent, ("x", "zr", "c"), 0, 0, tiled=True)
    return pl.pallas_call(
        place_kernel,
        out_shape=jax.ShapeDtypeStruct((OWN, 64, LANES), F32),
        scratch_shapes=[pltpu.VMEM((16 * 4 * SLOT, LANES), F32)],
        compiler_params=PARAMS,
        name="place",
    )(came)


def solution(mesh):
    fine = Mesh(mesh.devices.reshape(ZH, Y, X, ZQ, ZR, C), ("zh", "y") + TILE_AXES)
    in_specs = (P(TILE_AXES, ("zh", "y"), None), P(), P(TILE_AXES, None))
    out_specs = P(TILE_AXES, ("zh", "y"), None)
    return jax.shard_map(per_device, mesh=fine, in_specs=in_specs, out_specs=out_specs, check_vma=False)
```

```python
import math

import jax
import jax.numpy as jnp
import ml_dtypes
import numpy as np
from jax import lax
from jax.experimental import pallas as pl
from jax.experimental.pallas import tpu as pltpu
from jax.sharding import Mesh, PartitionSpec as P

NCHAN = 1024
QUARTER = NCHAN // 4
TIME = 48
TAPS = 4
FRAMES = 4 + TAPS - 1
LANES = 128
ZH, Y, X, ZQ, ZR, C = 2, 8, 4, 3, 2, 2
TILE_AXES = ("x", "zq", "zr", "c")
OWN = 11
SLOT = 12
VMEM = 48 * 1024 * 1024

BF = jnp.bfloat16
F32 = jnp.float32


def dft_table():
    zr, c, zh, x, y = np.meshgrid(*(np.arange(n) for n in (ZR, C, ZH, X, Y)), indexing="ij")
    first = ((zh * Y + y) * 64 + ((x * ZR + zr) * C + c) * 4).reshape(-1)
    channels = first[:, None] + np.arange(4)[None, :]
    products = channels[:, :, None] * np.arange(QUARTER)[None, None, :] % NCHAN
    angles = products.astype(np.float32) * np.float32(2.0 * math.pi / NCHAN)
    scale = np.float32(1.0 / math.sqrt(NCHAN))
    both = np.stack([np.cos(angles) * scale, np.sin(angles) * scale], axis=2)
    return both.reshape(256, 8 * QUARTER).astype(ml_dtypes.bfloat16)


def swap_chunks(rows, width):
    rows = list(rows)
    chunk = lax.broadcasted_iota(jnp.int32, rows[0].shape, 1) // width
    step = len(rows) // 2
    while step:
        low = (chunk & step) == 0
        for g in range(len(rows)):
            if not g & step:
                a, b = rows[g], rows[g + step]
                rows[g] = jnp.where(low, a, pltpu.roll(b, step * width, 1))
                rows[g + step] = jnp.where(low, pltpu.roll(a, LANES - step * width, 1), b)
        step //= 2
    return rows


def dot(a, b, contract):
    return lax.dot_general(a, b, ((contract[:1], contract[1:]), ((), ())), preferred_element_type=F32)


def split(value):
    high = value.astype(BF)
    return high, (value - high.astype(F32)).astype(BF)


def tap_kernel(map_hbm, volts_hbm, fir_hbm, table_hbm, out_ref, map_ref, volts_ref, fir_ref, table_ref, sems):
    pairs = ((volts_hbm.at[0], volts_ref), (fir_hbm, fir_ref), (map_hbm, map_ref), (table_hbm, table_ref))
    copies = [pltpu.make_async_copy(src, dst, sems.at[i]) for i, (src, dst) in enumerate(pairs)]
    for copy in copies:
        copy.start()
    copies[0].wait()
    copies[1].wait()
    lives = [[] for _ in range(4)]
    for k in range(TAPS):
        re, im = [], []
        for p, parts in enumerate((re, im)):
            for q in range(4):
                at = q * QUARTER
                part = volts_ref[:, p * NCHAN + at : p * NCHAN + at + QUARTER].astype(F32) * 0.25
                parts.append(fir_ref[k : k + 1, at : at + QUARTER] * part)
        evens = [(v[0] + v[2], v[1] + v[3]) for v in (re, im)]
        odds = [(v[0] - v[2], v[1] - v[3]) for v in (re, im)]
        sums = (
            (evens[0][0] + evens[0][1], evens[1][0] + evens[1][1]),
            (odds[0][0] + odds[1][1], odds[1][0] - odds[0][1]),
            (evens[0][0] - evens[0][1], evens[1][0] - evens[1][1]),
            (odds[0][0] - odds[1][1], odds[1][0] + odds[0][1]),
        )
        for j, (r, m) in enumerate(sums):
            lives[j] += [jnp.concatenate([r, m], axis=1), jnp.concatenate([m, -r], axis=1)]
    copies[3].wait()
    outs = []
    for j in range(4):
        table = table_ref[:, j * 2 * QUARTER : (j + 1) * 2 * QUARTER]
        high, low = split(jnp.concatenate(lives[j], axis=0))
        outs.append(dot(table, high, (1, 1)) + dot(table, low, (1, 1)))
    for k, part in enumerate(swap_chunks(outs, 32)):
        for j in range(ZR * C):
            out_ref[j, k * 64 : (k + 1) * 64, :] = part[j * 64 : (j + 1) * 64].astype(BF)

    copies[2].wait()
    sub = lax.broadcasted_iota(jnp.int32, (8, LANES), 0)
    lane = lax.broadcasted_iota(jnp.int32, (8, LANES), 1)
    place = lane - (lax.axis_index("zr") * C + lax.axis_index("c")) * SLOT
    tiles = jnp.zeros((8, LANES), jnp.int32)
    for l in range(OWN):
        tiles = jnp.where(place == l, map_ref[0, l], tiles)
        tiles = jnp.where(place == l + 64, map_ref[1, l], tiles)
    tiles = jnp.where(sub == 0, tiles, 0).astype(F32).astype(BF)
    for j in range(ZR * C):
        out_ref[j, 256:264, :] = tiles


def sum_kernel(in_ref, out_ref, f_ref):
    for f in range(FRAMES):
        total = None
        for k in range(TAPS):
            if 0 <= f - k < 4:
                part = in_ref[f - k, k * 64 : (k + 1) * 64, :].astype(F32)
                total = part if total is None else total + part
        for zh in range(ZH):
            f_ref[pl.ds(zh * FRAMES + f, X * Y, stride=16), :] = total[zh * X * Y : (zh + 1) * X * Y]
    tiles = sum(in_ref[j, 256:264, :].astype(F32) for j in range(ZR * C))
    f_ref[pl.ds(14, X * Y, stride=16), :] = jnp.broadcast_to(tiles[0:1], (X * Y, LANES))
    f_ref[pl.ds(15, X * Y, stride=16), :] = jnp.zeros((X * Y, LANES), F32)
    out_ref[...] = f_ref[...].reshape(X * Y, 16, LANES).astype(BF)


def turn_kernel(in_ref, out_ref, tiles_ref, f_ref):
    f_ref[...] = in_ref[...].astype(F32).reshape(f_ref.shape)
    for zh in range(ZH):
        for f in range(FRAMES):
            rows = f_ref[pl.ds(zh * FRAMES + f, X * Y, stride=16), :].astype(BF)
            for zq in range(ZQ):
                out_ref[zh * ZQ + zq, f * X * Y : (f + 1) * X * Y, :] = rows
    tiles_ref[...] = f_ref[pl.ds(14, X, stride=16 * Y), :]


def correlate_kernel(in_ref, tiles_ref, out_ref, f_ref, a_ref, c_ref, d_ref):
    def part(zh, zq, f):
        return in_ref[zh * ZQ + zq, f * 32 : (f + 1) * 32, :].astype(F32)

    for zh in range(ZH):
        for zq in range(ZQ):
            for f in range(4):
                rows = part(zh, zq, f)
                if f + 4 < FRAMES:
                    if zq:
                        rows = rows + part(zh, zq - 1, f + 4)
                    else:
                        spill = part(zh, ZQ - 1, f + 4)
                        rows = rows + jnp.concatenate([jnp.zeros((Y, LANES), F32), spill[: 32 - Y]], axis=0)
                f_ref[((zh * ZQ + zq) * 4 + f) * 32 : ((zh * ZQ + zq) * 4 + f + 1) * 32, :] = rows
    for zh in range(ZH):
        groups = [f_ref[pl.ds(zh * 384 + y, TIME, stride=Y), :] for y in range(Y)]
        for k, rows in enumerate(swap_chunks(groups, 16)):
            ch, p = divmod(k, 2)
            a_ref[ch, p * TIME : (p + 1) * TIME, zh * LANES : (zh + 1) * LANES] = rows.astype(BF)

    i = lax.broadcasted_iota(jnp.int32, (256, 256), 0)
    j = lax.broadcasted_iota(jnp.int32, (256, 256), 1)
    order = jnp.where(i == (j % 32) * 8 + j // 32, 1.0, 0.0).astype(BF)
    for ch in range(4):
        cols = a_ref[ch]
        left = dot(cols, order, (1, 0))
        re, im = left[:TIME], left[TIME:]
        both = jnp.concatenate([jnp.concatenate([re, im], axis=0), jnp.concatenate([im, -re], axis=0)], axis=1)
        c_ref[...] = dot(both.astype(BF), cols, (0, 0)) * (1.0 / TIME)
        for block, (h, g) in enumerate(((0, 0), (1, 0), (1, 1))):
            rows = [c_ref[k * 32 + g * 16 : k * 32 + g * 16 + 16, h * LANES : (h + 1) * LANES] for k in range(16)]
            for s, part in enumerate(swap_chunks(rows, 8)):
                at = block * 256 + s * 16
                d_ref[at : at + 16, ch * LANES : (ch + 1) * LANES] = part.astype(BF)

    lane = lax.broadcasted_iota(jnp.int32, (8, LANES), 1)
    firsts, seconds = [], []
    for half in range(2):
        for shift, found in ((0, firsts), (64, seconds)):
            total = None
            for x in range(2):
                rows = jnp.broadcast_to(tiles_ref[half * 2 + x : half * 2 + x + 1, :], (8, LANES))
                rows = pltpu.roll(rows, shift, 1) if shift else rows
                rows = jnp.where(lane < 4 * SLOT, rows, 0.0)
                total = rows if total is None else total + pltpu.roll(rows, x * 4 * SLOT, 1)
            found.append(total[0:1])
    r = jnp.concatenate(firsts, axis=1).astype(jnp.int32)
    s = jnp.concatenate(seconds, axis=1).astype(jnp.int32)
    rh, sh = jnp.where(r >= 16, 1, 0), jnp.where(s >= 16, 1, 0)
    index = (rh + sh) * 256 + (s - 16 * sh) * 16 + (r - 16 * rh)
    pick = jnp.where(lax.broadcasted_iota(jnp.int32, (768, 256), 0) == index, 1.0, 0.0).astype(BF)
    c_ref[:256, :] = dot(pick, d_ref[:, :256], (0, 0))
    c_ref[256:, :] = dot(pick, d_ref[:, 256:], (0, 0))
    for d in range(16):
        for ch in range(4):
            at = (ch // 2) * 256 + (d // 8) * LANES + (d % 8) * SLOT
            rows = c_ref[at : at + SLOT, (ch % 2) * LANES : (ch % 2 + 1) * LANES]
            f_ref[d * 48 + ch * SLOT : d * 48 + (ch + 1) * SLOT, :] = rows
    out_ref[...] = f_ref[...].reshape(16, 48, LANES).astype(BF)


def place_kernel(in_ref, out_ref, f_ref):
    f_ref[...] = in_ref[...].astype(F32).reshape(f_ref.shape)
    for l in range(OWN):
        out_ref[l] = f_ref[pl.ds(l, 64, stride=SLOT), :]


PARAMS = pltpu.CompilerParams(vmem_limit_bytes=VMEM)


def per_device(voltages, fir_taps, tile_map):
    hbm = pl.BlockSpec(memory_space=pltpu.MemorySpace.HBM)
    arrays = (tile_map.T, voltages, fir_taps, jnp.asarray(dft_table()))
    sent = pl.pallas_call(
        tap_kernel,
        out_shape=jax.ShapeDtypeStruct((ZR * C, 264, LANES), BF),
        in_specs=[hbm] * 4,
        scratch_shapes=[
            pltpu.SMEM((2, OWN), jnp.int32),
            pltpu.VMEM((16, 2 * NCHAN), jnp.int32),
            pltpu.VMEM((TAPS, NCHAN), F32),
            pltpu.VMEM((256, 8 * QUARTER), BF),
            pltpu.SemaphoreType.DMA((4,)),
        ],
        compiler_params=PARAMS,
        name="taps",
    )(*(pltpu.with_memory_space_constraint(a, pltpu.MemorySpace.HBM) for a in arrays))
    came = lax.all_to_all(sent, ("zr", "c"), 0, 0, tiled=True)
    sent = pl.pallas_call(
        sum_kernel,
        out_shape=jax.ShapeDtypeStruct((X * Y, 16, LANES), BF),
        scratch_shapes=[pltpu.VMEM((X * Y * 16, LANES), F32)],
        compiler_params=PARAMS,
        name="sum",
    )(came)
    came = lax.all_to_all(sent, ("x", "y"), 0, 0, tiled=True)
    sent, tiles = pl.pallas_call(
        turn_kernel,
        out_shape=(
            jax.ShapeDtypeStruct((ZH * ZQ, FRAMES * X * Y, LANES), BF),
            jax.ShapeDtypeStruct((X, LANES), F32),
        ),
        scratch_shapes=[pltpu.VMEM((X * Y * 16, LANES), F32)],
        compiler_params=PARAMS,
        name="turn",
    )(came)
    came = lax.all_to_all(sent, ("zh", "zq"), 0, 0, tiled=True)
    sent = pl.pallas_call(
        correlate_kernel,
        out_shape=jax.ShapeDtypeStruct((16, 4 * SLOT, LANES), BF),
        scratch_shapes=[
            pltpu.VMEM((768, LANES), F32),
            pltpu.VMEM((4, 2 * TIME, 256), BF),
            pltpu.VMEM((512, 256), F32),
            pltpu.VMEM((768, 512), BF),
        ],
        compiler_params=PARAMS,
        name="correlate",
    )(came, tiles)
    came = lax.all_to_all(sent, ("x", "zr", "c"), 0, 0, tiled=True)
    return pl.pallas_call(
        place_kernel,
        out_shape=jax.ShapeDtypeStruct((OWN, 64, LANES), F32),
        scratch_shapes=[pltpu.VMEM((16 * 4 * SLOT, LANES), F32)],
        compiler_params=PARAMS,
        name="place",
    )(came)


def solution(mesh):
    fine = Mesh(mesh.devices.reshape(ZH, Y, X, ZQ, ZR, C), ("zh", "y") + TILE_AXES)
    in_specs = (P(TILE_AXES, ("zh", "y"), None), P(), P(TILE_AXES, None))
    out_specs = P(TILE_AXES, ("zh", "y"), None)
    return jax.shard_map(per_device, mesh=fine, in_specs=in_specs, out_specs=out_specs, check_vma=False)
```

```python
import math

import jax
import jax.numpy as jnp
import ml_dtypes
import numpy as np
from jax import lax
from jax.experimental import pallas as pl
from jax.experimental.pallas import tpu as pltpu
from jax.sharding import Mesh, PartitionSpec as P

NCHAN = 1024
QUARTER = NCHAN // 4
TIME = 48
TAPS = 4
FRAMES = 4 + TAPS - 1
LANES = 128
ZH, Y, X, ZQ, ZR, C = 2, 8, 4, 3, 2, 2
TILE_AXES = ("x", "zq", "zr", "c")
OWN = 11
SLOT = 12
VMEM = 48 * 1024 * 1024

BF = jnp.bfloat16
F32 = jnp.float32


def dft_table():
    x, zr, c, zh, y = np.meshgrid(*(np.arange(n) for n in (X, ZR, C, ZH, Y)), indexing="ij")
    first = ((zh * Y + y) * 64 + ((x * ZR + zr) * C + c) * 4).reshape(-1)
    channels = first[:, None] + np.arange(4)[None, :]
    products = channels[:, :, None] * np.arange(QUARTER)[None, None, :] % NCHAN
    angles = products.astype(np.float32) * np.float32(2.0 * math.pi / NCHAN)
    scale = np.float32(1.0 / math.sqrt(NCHAN))
    both = np.stack([np.cos(angles) * scale, np.sin(angles) * scale], axis=2)
    return both.reshape(256, 8 * QUARTER).astype(ml_dtypes.bfloat16)


def swap_chunks(rows, width):
    rows = list(rows)
    chunk = lax.broadcasted_iota(jnp.int32, rows[0].shape, 1) // width
    step = len(rows) // 2
    while step:
        low = (chunk & step) == 0
        for g in range(len(rows)):
            if not g & step:
                a, b = rows[g], rows[g + step]
                rows[g] = jnp.where(low, a, pltpu.roll(b, step * width, 1))
                rows[g + step] = jnp.where(low, pltpu.roll(a, LANES - step * width, 1), b)
        step //= 2
    return rows


def dot(a, b, contract):
    return lax.dot_general(a, b, ((contract[:1], contract[1:]), ((), ())), preferred_element_type=F32)


def split(value):
    high = value.astype(BF)
    return high, (value - high.astype(F32)).astype(BF)


def tap_kernel(map_hbm, volts_hbm, fir_hbm, table_hbm, out_ref, map_ref, volts_ref, fir_ref, table_ref, sems):
    pairs = ((volts_hbm.at[0], volts_ref), (fir_hbm, fir_ref), (map_hbm, map_ref), (table_hbm, table_ref))
    copies = [pltpu.make_async_copy(src, dst, sems.at[i]) for i, (src, dst) in enumerate(pairs)]
    for copy in copies:
        copy.start()
    copies[0].wait()
    copies[1].wait()
    lives = [[] for _ in range(4)]
    for k in range(TAPS):
        re, im = [], []
        for p, parts in enumerate((re, im)):
            for q in range(4):
                at = q * QUARTER
                part = volts_ref[:, p * NCHAN + at : p * NCHAN + at + QUARTER].astype(F32) * 0.25
                parts.append(fir_ref[k : k + 1, at : at + QUARTER] * part)
        evens = [(v[0] + v[2], v[1] + v[3]) for v in (re, im)]
        odds = [(v[0] - v[2], v[1] - v[3]) for v in (re, im)]
        sums = (
            (evens[0][0] + evens[0][1], evens[1][0] + evens[1][1]),
            (odds[0][0] + odds[1][1], odds[1][0] - odds[0][1]),
            (evens[0][0] - evens[0][1], evens[1][0] - evens[1][1]),
            (odds[0][0] - odds[1][1], odds[1][0] + odds[0][1]),
        )
        for j, (r, m) in enumerate(sums):
            lives[j] += [jnp.concatenate([r, m], axis=1), jnp.concatenate([m, -r], axis=1)]
    copies[3].wait()
    outs = []
    for j in range(4):
        table = table_ref[:, j * 2 * QUARTER : (j + 1) * 2 * QUARTER]
        high, low = split(jnp.concatenate(lives[j], axis=0))
        outs.append(dot(table, high, (1, 1)) + dot(table, low, (1, 1)))
    for k, part in enumerate(swap_chunks(outs, 32)):
        out_ref[:, k * 16 : (k + 1) * 16, :] = part.astype(BF).reshape(16, 16, LANES)

    copies[2].wait()
    sub = lax.broadcasted_iota(jnp.int32, (8, LANES), 0)
    lane = lax.broadcasted_iota(jnp.int32, (8, LANES), 1)
    own = (lax.axis_index("x") * ZR + lax.axis_index("zr")) * C + lax.axis_index("c")
    place = lane + (sub % 2) * (8 * SLOT) - own * SLOT
    tiles = jnp.zeros((8, LANES), jnp.int32)
    for l in range(OWN):
        tiles = jnp.where(place == l, jnp.where(sub < 2, map_ref[0, l], map_ref[1, l]), tiles)
    tiles = jnp.where((sub < 4) & (lane < 8 * SLOT), tiles, 0).astype(F32).astype(BF)
    for d in range(16):
        out_ref[d, 64:72, :] = tiles


def sum_kernel(in_ref, out_ref, tiles_ref, f_ref):
    zq = lax.axis_index("zq")
    sums = [[None] * (FRAMES + 1) for _ in range(X)]
    for x in range(X):
        for f in range(FRAMES):
            for k in range(TAPS):
                if 0 <= f - k < 4:
                    part = in_ref[x * 4 + f - k, k * 16 : (k + 1) * 16, :].astype(F32)
                    sums[x][f] = part if sums[x][f] is None else sums[x][f] + part
        sums[x][FRAMES] = jnp.zeros((16, LANES), F32)
    zeros = jnp.zeros((16, LANES), F32)
    for spill in range(2):
        for x in range(X):
            for f in range(4):
                rows = sums[x][4 * spill + f]
                if spill:
                    rows = jnp.where(zq == ZQ - 1, sums[x - 1][4 + f] if x else zeros, rows)
                for zh in range(ZH):
                    at = spill * 256 + zh * 16 + x * 4 + f
                    f_ref[pl.ds(at, Y, stride=32), :] = rows[zh * Y : (zh + 1) * Y]
    out_ref[zq] = f_ref[:256, :].reshape(Y, 32, LANES).astype(BF)
    out_ref[lax.rem(zq + 1, ZQ)] = f_ref[256:, :].reshape(Y, 32, LANES).astype(BF)
    out_ref[lax.rem(zq + 2, ZQ)] = jnp.zeros((Y, 32, LANES), BF)
    tiles_ref[...] = sum(in_ref[d, 64:72, :].astype(F32) for d in range(16))


def turn_kernel(in_ref, out_ref, f_ref):
    zq = lax.axis_index("zq")
    both = in_ref[zq].astype(F32) + in_ref[lax.rem(zq + 2, ZQ)].astype(F32)
    f_ref[...] = both.reshape(f_ref.shape)
    for zh in range(ZH):
        rows = [f_ref[pl.ds(zh * 16 + k, Y, stride=32), :] for k in range(16)]
        block = jnp.concatenate(rows, axis=0).astype(BF)
        for q in range(ZQ):
            out_ref[zh * ZQ + q] = block


def correlate_kernel(in_ref, tiles_ref, out_ref, f_ref, a_ref, c_ref, d_ref):
    f_ref[...] = in_ref[...].astype(F32).reshape(f_ref.shape)
    for zh in range(ZH):
        groups = [f_ref[pl.ds(zh * 384 + y, TIME, stride=Y), :] for y in range(Y)]
        for k, rows in enumerate(swap_chunks(groups, 16)):
            ch, p = divmod(k, 2)
            a_ref[ch, p * TIME : (p + 1) * TIME, zh * LANES : (zh + 1) * LANES] = rows.astype(BF)

    i = lax.broadcasted_iota(jnp.int32, (256, 256), 0)
    j = lax.broadcasted_iota(jnp.int32, (256, 256), 1)
    order = jnp.where(i == (j % 32) * 8 + j // 32, 1.0, 0.0).astype(BF)
    for ch in range(4):
        cols = a_ref[ch]
        left = dot(cols, order, (1, 0))
        re, im = left[:TIME], left[TIME:]
        both = jnp.concatenate([jnp.concatenate([re, im], axis=0), jnp.concatenate([im, -re], axis=0)], axis=1)
        c_ref[...] = dot(both.astype(BF), cols, (0, 0)) * (1.0 / TIME)
        for block, (h, g) in enumerate(((0, 0), (1, 0), (1, 1))):
            rows = [c_ref[k * 32 + g * 16 : k * 32 + g * 16 + 16, h * LANES : (h + 1) * LANES] for k in range(16)]
            for s, part in enumerate(swap_chunks(rows, 8)):
                at = block * 256 + s * 16
                d_ref[at : at + 16, ch * LANES : (ch + 1) * LANES] = part.astype(BF)

    r = jnp.concatenate([tiles_ref[0:1], tiles_ref[1:2]], axis=1).astype(jnp.int32)
    s = jnp.concatenate([tiles_ref[2:3], tiles_ref[3:4]], axis=1).astype(jnp.int32)
    rh, sh = jnp.where(r >= 16, 1, 0), jnp.where(s >= 16, 1, 0)
    index = (rh + sh) * 256 + (s - 16 * sh) * 16 + (r - 16 * rh)
    pick = jnp.where(lax.broadcasted_iota(jnp.int32, (768, 256), 0) == index, 1.0, 0.0).astype(BF)
    c_ref[:256, :] = dot(pick, d_ref[:, :256], (0, 0))
    c_ref[256:, :] = dot(pick, d_ref[:, 256:], (0, 0))
    for d in range(16):
        for ch in range(4):
            at = (ch // 2) * 256 + (d // 8) * LANES + (d % 8) * SLOT
            rows = c_ref[at : at + SLOT, (ch % 2) * LANES : (ch % 2 + 1) * LANES]
            f_ref[d * 48 + ch * SLOT : d * 48 + (ch + 1) * SLOT, :] = rows
    out_ref[...] = f_ref[...].reshape(16, 48, LANES).astype(BF)


def place_kernel(in_ref, out_ref, f_ref):
    f_ref[...] = in_ref[...].astype(F32).reshape(f_ref.shape)
    for l in range(OWN):
        out_ref[l] = f_ref[pl.ds(l, 64, stride=SLOT), :]


PARAMS = pltpu.CompilerParams(vmem_limit_bytes=VMEM)


def per_device(voltages, fir_taps, tile_map):
    hbm = pl.BlockSpec(memory_space=pltpu.MemorySpace.HBM)
    arrays = (tile_map.T, voltages, fir_taps, jnp.asarray(dft_table()))
    sent = pl.pallas_call(
        tap_kernel,
        out_shape=jax.ShapeDtypeStruct((X * ZR * C, 72, LANES), BF),
        in_specs=[hbm] * 4,
        scratch_shapes=[
            pltpu.SMEM((2, OWN), jnp.int32),
            pltpu.VMEM((16, 2 * NCHAN), jnp.int32),
            pltpu.VMEM((TAPS, NCHAN), F32),
            pltpu.VMEM((256, 8 * QUARTER), BF),
            pltpu.SemaphoreType.DMA((4,)),
        ],
        compiler_params=PARAMS,
        name="taps",
    )(*(pltpu.with_memory_space_constraint(a, pltpu.MemorySpace.HBM) for a in arrays))
    came = lax.all_to_all(sent, ("x", "zr", "c"), 0, 0, tiled=True)
    sent, tiles = pl.pallas_call(
        sum_kernel,
        out_shape=(
            jax.ShapeDtypeStruct((ZQ, Y, 32, LANES), BF),
            jax.ShapeDtypeStruct((8, LANES), F32),
        ),
        scratch_shapes=[pltpu.VMEM((512, LANES), F32)],
        compiler_params=PARAMS,
        name="sum",
    )(came)
    came = lax.all_to_all(sent.reshape(ZQ * Y, 32, LANES), ("zq", "y"), 0, 0, tiled=True)
    sent = pl.pallas_call(
        turn_kernel,
        out_shape=jax.ShapeDtypeStruct((ZH * ZQ, 128, LANES), BF),
        scratch_shapes=[pltpu.VMEM((256, LANES), F32)],
        compiler_params=PARAMS,
        name="turn",
    )(came.reshape(ZQ, Y, 32, LANES))
    came = lax.all_to_all(sent, ("zh", "zq"), 0, 0, tiled=True)
    sent = pl.pallas_call(
        correlate_kernel,
        out_shape=jax.ShapeDtypeStruct((16, 4 * SLOT, LANES), BF),
        scratch_shapes=[
            pltpu.VMEM((768, LANES), F32),
            pltpu.VMEM((4, 2 * TIME, 256), BF),
            pltpu.VMEM((512, 256), F32),
            pltpu.VMEM((768, 512), BF),
        ],
        compiler_params=PARAMS,
        name="correlate",
    )(came, tiles)
    came = lax.all_to_all(sent, ("x", "zr", "c"), 0, 0, tiled=True)
    return pl.pallas_call(
        place_kernel,
        out_shape=jax.ShapeDtypeStruct((OWN, 64, LANES), F32),
        scratch_shapes=[pltpu.VMEM((16 * 4 * SLOT, LANES), F32)],
        compiler_params=PARAMS,
        name="place",
    )(came)


def solution(mesh):
    fine = Mesh(mesh.devices.reshape(ZH, Y, X, ZQ, ZR, C), ("zh", "y") + TILE_AXES)
    in_specs = (P(TILE_AXES, ("zh", "y"), None), P(), P(TILE_AXES, None))
    out_specs = P(TILE_AXES, ("zh", "y"), None)
    return jax.shard_map(per_device, mesh=fine, in_specs=in_specs, out_specs=out_specs, check_vma=False)
```

```python
import math

import jax
import jax.numpy as jnp
import ml_dtypes
import numpy as np
from jax import lax
from jax.experimental import pallas as pl
from jax.experimental.pallas import tpu as pltpu
from jax.sharding import Mesh, PartitionSpec as P

NCHAN = 1024
QUARTER = NCHAN // 4
TIME = 48
TAPS = 4
FRAMES = 4 + TAPS - 1
LANES = 128
ZH, Y, X, ZQ, ZR, C = 2, 8, 4, 3, 2, 2
TILE_AXES = ("x", "zq", "zr", "c")
OWN = 11
SLOT = 12
VMEM = 48 * 1024 * 1024

BF = jnp.bfloat16
F32 = jnp.float32


def dft_table():
    x, zr, c, zh, y = np.meshgrid(*(np.arange(n) for n in (X, ZR, C, ZH, Y)), indexing="ij")
    first = ((zh * Y + y) * 64 + ((x * ZR + zr) * C + c) * 4).reshape(-1)
    channels = first[:, None] + np.arange(4)[None, :]
    products = channels[:, :, None] * np.arange(QUARTER)[None, None, :] % NCHAN
    angles = products.astype(np.float32) * np.float32(2.0 * math.pi / NCHAN)
    scale = np.float32(1.0 / math.sqrt(NCHAN))
    both = np.stack([np.cos(angles) * scale, np.sin(angles) * scale], axis=2)
    return both.reshape(256, 8 * QUARTER).astype(ml_dtypes.bfloat16)


def swap_chunks(rows, width):
    rows = list(rows)
    chunk = lax.broadcasted_iota(jnp.int32, rows[0].shape, 1) // width
    step = len(rows) // 2
    while step:
        low = (chunk & step) == 0
        for g in range(len(rows)):
            if not g & step:
                a, b = rows[g], rows[g + step]
                rows[g] = jnp.where(low, a, pltpu.roll(b, step * width, 1))
                rows[g + step] = jnp.where(low, pltpu.roll(a, LANES - step * width, 1), b)
        step //= 2
    return rows


def dot(a, b, contract):
    return lax.dot_general(a, b, ((contract[:1], contract[1:]), ((), ())), preferred_element_type=F32)


def split(value):
    high = value.astype(BF)
    return high, (value - high.astype(F32)).astype(BF)


def tap_kernel(map_hbm, volts_hbm, fir_hbm, table_hbm, out_ref, map_ref, volts_ref, fir_ref, table_ref, sems):
    pairs = ((volts_hbm.at[0], volts_ref), (fir_hbm, fir_ref), (map_hbm, map_ref), (table_hbm, table_ref))
    copies = [pltpu.make_async_copy(src, dst, sems.at[i]) for i, (src, dst) in enumerate(pairs)]
    for copy in copies:
        copy.start()
    copies[0].wait()
    copies[1].wait()
    lives = [[] for _ in range(4)]
    for k in range(TAPS):
        re, im = [], []
        for p, parts in enumerate((re, im)):
            for q in range(4):
                at = q * QUARTER
                part = volts_ref[:, p * NCHAN + at : p * NCHAN + at + QUARTER].astype(F32) * 0.25
                parts.append(fir_ref[k : k + 1, at : at + QUARTER] * part)
        evens = [(v[0] + v[2], v[1] + v[3]) for v in (re, im)]
        odds = [(v[0] - v[2], v[1] - v[3]) for v in (re, im)]
        sums = (
            (evens[0][0] + evens[0][1], evens[1][0] + evens[1][1]),
            (odds[0][0] + odds[1][1], odds[1][0] - odds[0][1]),
            (evens[0][0] - evens[0][1], evens[1][0] - evens[1][1]),
            (odds[0][0] - odds[1][1], odds[1][0] + odds[0][1]),
        )
        for j, (r, m) in enumerate(sums):
            lives[j] += [jnp.concatenate([r, m], axis=1), jnp.concatenate([m, -r], axis=1)]
    copies[3].wait()
    outs = []
    for j in range(4):
        table = table_ref[:, j * 2 * QUARTER : (j + 1) * 2 * QUARTER]
        high, low = split(jnp.concatenate(lives[j], axis=0))
        outs.append(dot(table, high, (1, 1)) + dot(table, low, (1, 1)))
    for k, part in enumerate(swap_chunks(outs, 32)):
        out_ref[:, k * 16 : (k + 1) * 16, :] = part.astype(BF).reshape(16, 16, LANES)

    copies[2].wait()
    sub = lax.broadcasted_iota(jnp.int32, (8, LANES), 0)
    lane = lax.broadcasted_iota(jnp.int32, (8, LANES), 1)
    own = (lax.axis_index("x") * ZR + lax.axis_index("zr")) * C + lax.axis_index("c")
    place = lane + (sub % 2) * (8 * SLOT) - own * SLOT
    tiles = jnp.zeros((8, LANES), jnp.int32)
    for l in range(OWN):
        tiles = jnp.where(place == l, jnp.where(sub < 2, map_ref[0, l], map_ref[1, l]), tiles)
    tiles = jnp.where((sub < 4) & (lane < 8 * SLOT), tiles, 0).astype(F32).astype(BF)
    for d in range(16):
        out_ref[d, 64:72, :] = tiles


def sum_kernel(in_ref, out_ref, tiles_ref, f_ref):
    for x in range(X):
        for f in range(FRAMES):
            total = None
            for k in range(TAPS):
                if 0 <= f - k < 4:
                    part = in_ref[x * 4 + f - k, k * 16 : (k + 1) * 16, :].astype(F32)
                    total = part if total is None else total + part
            for zh in range(ZH):
                f_ref[pl.ds((zh * X + x) * FRAMES + f, Y, stride=56), :] = total[zh * Y : (zh + 1) * Y]
    out_ref[...] = f_ref[...].reshape(Y, 56, LANES).astype(BF)
    tiles_ref[...] = sum(in_ref[d, 64:72, :].astype(F32) for d in range(16))


def turn_kernel(in_ref, out_ref, f_ref):
    f_ref[...] = in_ref[...].astype(F32).reshape(f_ref.shape)
    for zh in range(ZH):
        for f in range(FRAMES):
            rows = [f_ref[pl.ds((zh * X + x) * FRAMES + f, Y, stride=56), :] for x in range(X)]
            block = jnp.concatenate(rows, axis=0).astype(BF)
            for zq in range(ZQ):
                out_ref[zh * ZQ + zq, f * 32 : (f + 1) * 32, :] = block


def correlate_kernel(in_ref, tiles_ref, out_ref, f_ref, a_ref, c_ref, d_ref):
    def part(zh, zq, f):
        return in_ref[zh * ZQ + zq, f * 32 : (f + 1) * 32, :].astype(F32)

    for zh in range(ZH):
        for zq in range(ZQ):
            for f in range(4):
                rows = part(zh, zq, f)
                if f + 4 < FRAMES:
                    if zq:
                        rows = rows + part(zh, zq - 1, f + 4)
                    else:
                        spill = part(zh, ZQ - 1, f + 4)
                        rows = rows + jnp.concatenate([jnp.zeros((Y, LANES), F32), spill[: 32 - Y]], axis=0)
                f_ref[((zh * ZQ + zq) * 4 + f) * 32 : ((zh * ZQ + zq) * 4 + f + 1) * 32, :] = rows
    for zh in range(ZH):
        groups = [f_ref[pl.ds(zh * 384 + y, TIME, stride=Y), :] for y in range(Y)]
        for k, rows in enumerate(swap_chunks(groups, 16)):
            ch, p = divmod(k, 2)
            a_ref[ch, p * TIME : (p + 1) * TIME, zh * LANES : (zh + 1) * LANES] = rows.astype(BF)

    i = lax.broadcasted_iota(jnp.int32, (256, 256), 0)
    j = lax.broadcasted_iota(jnp.int32, (256, 256), 1)
    order = jnp.where(i == (j % 32) * 8 + j // 32, 1.0, 0.0).astype(BF)
    for ch in range(4):
        cols = a_ref[ch]
        left = dot(cols, order, (1, 0))
        re, im = left[:TIME], left[TIME:]
        both = jnp.concatenate([jnp.concatenate([re, im], axis=0), jnp.concatenate([im, -re], axis=0)], axis=1)
        c_ref[...] = dot(both.astype(BF), cols, (0, 0)) * (1.0 / TIME)
        for block, (h, g) in enumerate(((0, 0), (1, 0), (1, 1))):
            rows = [c_ref[k * 32 + g * 16 : k * 32 + g * 16 + 16, h * LANES : (h + 1) * LANES] for k in range(16)]
            for s, part in enumerate(swap_chunks(rows, 8)):
                at = block * 256 + s * 16
                d_ref[at : at + 16, ch * LANES : (ch + 1) * LANES] = part.astype(BF)

    r = jnp.concatenate([tiles_ref[0:1], tiles_ref[1:2]], axis=1).astype(jnp.int32)
    s = jnp.concatenate([tiles_ref[2:3], tiles_ref[3:4]], axis=1).astype(jnp.int32)
    rh, sh = jnp.where(r >= 16, 1, 0), jnp.where(s >= 16, 1, 0)
    index = (rh + sh) * 256 + (s - 16 * sh) * 16 + (r - 16 * rh)
    pick = jnp.where(lax.broadcasted_iota(jnp.int32, (768, 256), 0) == index, 1.0, 0.0).astype(BF)
    c_ref[:256, :] = dot(pick, d_ref[:, :256], (0, 0))
    c_ref[256:, :] = dot(pick, d_ref[:, 256:], (0, 0))
    for d in range(16):
        for ch in range(4):
            at = (ch // 2) * 256 + (d // 8) * LANES + (d % 8) * SLOT
            rows = c_ref[at : at + SLOT, (ch % 2) * LANES : (ch % 2 + 1) * LANES]
            f_ref[d * 48 + ch * SLOT : d * 48 + (ch + 1) * SLOT, :] = rows
    out_ref[...] = f_ref[...].reshape(16, 48, LANES).astype(BF)


def place_kernel(in_ref, out_ref, f_ref):
    f_ref[...] = in_ref[...].astype(F32).reshape(f_ref.shape)
    for l in range(OWN):
        out_ref[l] = f_ref[pl.ds(l, 64, stride=SLOT), :]


PARAMS = pltpu.CompilerParams(vmem_limit_bytes=VMEM)


def per_device(voltages, fir_taps, tile_map):
    hbm = pl.BlockSpec(memory_space=pltpu.MemorySpace.HBM)
    arrays = (tile_map.T, voltages, fir_taps, jnp.asarray(dft_table()))
    sent = pl.pallas_call(
        tap_kernel,
        out_shape=jax.ShapeDtypeStruct((X * ZR * C, 72, LANES), BF),
        in_specs=[hbm] * 4,
        scratch_shapes=[
            pltpu.SMEM((2, OWN), jnp.int32),
            pltpu.VMEM((16, 2 * NCHAN), jnp.int32),
            pltpu.VMEM((TAPS, NCHAN), F32),
            pltpu.VMEM((256, 8 * QUARTER), BF),
            pltpu.SemaphoreType.DMA((4,)),
        ],
        compiler_params=PARAMS,
        name="taps",
    )(*(pltpu.with_memory_space_constraint(a, pltpu.MemorySpace.HBM) for a in arrays))
    came = lax.all_to_all(sent, ("x", "zr", "c"), 0, 0, tiled=True)
    sent, tiles = pl.pallas_call(
        sum_kernel,
        out_shape=(
            jax.ShapeDtypeStruct((Y, 56, LANES), BF),
            jax.ShapeDtypeStruct((8, LANES), F32),
        ),
        scratch_shapes=[pltpu.VMEM((Y * 56, LANES), F32)],
        compiler_params=PARAMS,
        name="sum",
    )(came)
    came = lax.all_to_all(sent, "y", 0, 0, tiled=True)
    sent = pl.pallas_call(
        turn_kernel,
        out_shape=jax.ShapeDtypeStruct((ZH * ZQ, FRAMES * X * Y, LANES), BF),
        scratch_shapes=[pltpu.VMEM((Y * 56, LANES), F32)],
        compiler_params=PARAMS,
        name="turn",
    )(came)
    came = lax.all_to_all(sent, ("zh", "zq"), 0, 0, tiled=True)
    sent = pl.pallas_call(
        correlate_kernel,
        out_shape=jax.ShapeDtypeStruct((16, 4 * SLOT, LANES), BF),
        scratch_shapes=[
            pltpu.VMEM((768, LANES), F32),
            pltpu.VMEM((4, 2 * TIME, 256), BF),
            pltpu.VMEM((512, 256), F32),
            pltpu.VMEM((768, 512), BF),
        ],
        compiler_params=PARAMS,
        name="correlate",
    )(came, tiles)
    came = lax.all_to_all(sent, ("x", "zr", "c"), 0, 0, tiled=True)
    return pl.pallas_call(
        place_kernel,
        out_shape=jax.ShapeDtypeStruct((OWN, 64, LANES), F32),
        scratch_shapes=[pltpu.VMEM((16 * 4 * SLOT, LANES), F32)],
        compiler_params=PARAMS,
        name="place",
    )(came)


def solution(mesh):
    fine = Mesh(mesh.devices.reshape(ZH, Y, X, ZQ, ZR, C), ("zh", "y") + TILE_AXES)
    in_specs = (P(TILE_AXES, ("zh", "y"), None), P(), P(TILE_AXES, None))
    out_specs = P(TILE_AXES, ("zh", "y"), None)
    return jax.shard_map(per_device, mesh=fine, in_specs=in_specs, out_specs=out_specs, check_vma=False)
```

```python
import math

import jax
import jax.numpy as jnp
import ml_dtypes
import numpy as np
from jax import lax
from jax.experimental import pallas as pl
from jax.experimental.pallas import tpu as pltpu
from jax.sharding import Mesh, PartitionSpec as P

NCHAN = 1024
QUARTER = NCHAN // 4
TIME = 48
TAPS = 4
FRAMES = 4 + TAPS - 1
LANES = 128
ZH, Y, X, ZQ, ZR, C = 2, 8, 4, 3, 2, 2
TILE_AXES = ("x", "zq", "zr", "c")
OWN = 11
SLOT = 12
VMEM = 48 * 1024 * 1024

BF = jnp.bfloat16
F32 = jnp.float32


def dft_table():
    x, zr, c, zh, y = np.meshgrid(*(np.arange(n) for n in (X, ZR, C, ZH, Y)), indexing="ij")
    first = ((zh * Y + y) * 64 + ((x * ZR + zr) * C + c) * 4).reshape(-1)
    channels = first[:, None] + np.arange(4)[None, :]
    products = channels[:, :, None] * np.arange(QUARTER)[None, None, :] % NCHAN
    angles = products.astype(np.float32) * np.float32(2.0 * math.pi / NCHAN)
    scale = np.float32(1.0 / math.sqrt(NCHAN))
    both = np.stack([np.cos(angles) * scale, np.sin(angles) * scale], axis=2)
    return both.reshape(256, 8 * QUARTER).astype(ml_dtypes.bfloat16)


def swap_chunks(rows, width):
    rows = list(rows)
    chunk = lax.broadcasted_iota(jnp.int32, rows[0].shape, 1) // width
    step = len(rows) // 2
    while step:
        low = (chunk & step) == 0
        for g in range(len(rows)):
            if not g & step:
                a, b = rows[g], rows[g + step]
                rows[g] = jnp.where(low, a, pltpu.roll(b, step * width, 1))
                rows[g + step] = jnp.where(low, pltpu.roll(a, LANES - step * width, 1), b)
        step //= 2
    return rows


def dot(a, b, contract):
    return lax.dot_general(a, b, ((contract[:1], contract[1:]), ((), ())), preferred_element_type=F32)


def split(value):
    high = value.astype(BF)
    return high, (value - high.astype(F32)).astype(BF)


def tap_kernel(map_hbm, volts_hbm, fir_hbm, table_hbm, out_ref, map_ref, volts_ref, fir_ref, table_ref, sems):
    pairs = ((volts_hbm.at[0], volts_ref), (fir_hbm, fir_ref), (map_hbm, map_ref), (table_hbm, table_ref))
    copies = [pltpu.make_async_copy(src, dst, sems.at[i]) for i, (src, dst) in enumerate(pairs)]
    for copy in copies:
        copy.start()
    copies[0].wait()
    copies[1].wait()
    lives = [[] for _ in range(4)]
    for k in range(TAPS):
        re, im = [], []
        for p, parts in enumerate((re, im)):
            for q in range(4):
                at = q * QUARTER
                part = volts_ref[:, p * NCHAN + at : p * NCHAN + at + QUARTER].astype(F32) * 0.25
                parts.append(fir_ref[k : k + 1, at : at + QUARTER] * part)
        evens = [(v[0] + v[2], v[1] + v[3]) for v in (re, im)]
        odds = [(v[0] - v[2], v[1] - v[3]) for v in (re, im)]
        sums = (
            (evens[0][0] + evens[0][1], evens[1][0] + evens[1][1]),
            (odds[0][0] + odds[1][1], odds[1][0] - odds[0][1]),
            (evens[0][0] - evens[0][1], evens[1][0] - evens[1][1]),
            (odds[0][0] - odds[1][1], odds[1][0] + odds[0][1]),
        )
        for j, (r, m) in enumerate(sums):
            lives[j] += [jnp.concatenate([r, m], axis=1), jnp.concatenate([m, -r], axis=1)]
    copies[3].wait()
    outs = []
    for j in range(4):
        table = table_ref[:, j * 2 * QUARTER : (j + 1) * 2 * QUARTER]
        high, low = split(jnp.concatenate(lives[j], axis=0))
        outs.append(dot(table, high, (1, 1)) + dot(table, low, (1, 1)))
    for k, part in enumerate(swap_chunks(outs, 32)):
        out_ref[:, k * 16 : (k + 1) * 16, :] = part.astype(BF).reshape(16, 16, LANES)

    copies[2].wait()
    sub = lax.broadcasted_iota(jnp.int32, (8, LANES), 0)
    lane = lax.broadcasted_iota(jnp.int32, (8, LANES), 1)
    own = (lax.axis_index("x") * ZR + lax.axis_index("zr")) * C + lax.axis_index("c")
    place = lane + (sub % 2) * (8 * SLOT) - own * SLOT
    tiles = jnp.zeros((8, LANES), jnp.int32)
    for l in range(OWN):
        tiles = jnp.where(place == l, jnp.where(sub < 2, map_ref[0, l], map_ref[1, l]), tiles)
    tiles = jnp.where((sub < 4) & (lane < 8 * SLOT), tiles, 0).astype(F32).astype(BF)
    for d in range(16):
        out_ref[d, 64:72, :] = tiles


def sum_kernel(in_ref, out_ref, tiles_ref, f_ref):
    for x in range(X):
        for f in range(FRAMES):
            total = None
            for k in range(TAPS):
                if 0 <= f - k < 4:
                    part = in_ref[x * 4 + f - k, k * 16 : (k + 1) * 16, :].astype(F32)
                    total = part if total is None else total + part
            for zh in range(ZH):
                f_ref[pl.ds((zh * X + x) * FRAMES + f, Y, stride=56), :] = total[zh * Y : (zh + 1) * Y]
    out_ref[...] = f_ref[...].reshape(Y, 56, LANES).astype(BF)
    tiles_ref[...] = sum(in_ref[d, 64:72, :].astype(F32) for d in range(16))


def turn_kernel(in_ref, out_ref, f_ref):
    f_ref[...] = in_ref[...].astype(F32).reshape(f_ref.shape)
    for zh in range(ZH):
        for f in range(FRAMES):
            rows = [f_ref[pl.ds((zh * X + x) * FRAMES + f, Y, stride=56), :] for x in range(X)]
            block = jnp.concatenate(rows, axis=0).astype(BF)
            for zq in range(ZQ):
                out_ref[zh * ZQ + zq, f * 32 : (f + 1) * 32, :] = block


def correlate_kernel(in_ref, tiles_ref, out_ref, f_ref, a_ref, c_ref, d_ref):
    def part(zh, zq, f):
        return in_ref[zh * ZQ + zq, f * 32 : (f + 1) * 32, :].astype(F32)

    for zh in range(ZH):
        for zq in range(ZQ):
            for f in range(4):
                rows = part(zh, zq, f)
                if f + 4 < FRAMES:
                    if zq:
                        rows = rows + part(zh, zq - 1, f + 4)
                    else:
                        spill = part(zh, ZQ - 1, f + 4)
                        rows = rows + jnp.concatenate([jnp.zeros((Y, LANES), F32), spill[: 32 - Y]], axis=0)
                f_ref[((zh * ZQ + zq) * 4 + f) * 32 : ((zh * ZQ + zq) * 4 + f + 1) * 32, :] = rows
    for zh in range(ZH):
        groups = [f_ref[pl.ds(zh * 384 + y, TIME, stride=Y), :] for y in range(Y)]
        for k, rows in enumerate(swap_chunks(groups, 16)):
            ch, p = divmod(k, 2)
            for h, half in enumerate(split(rows)):
                at = (2 * h + p) * TIME
                a_ref[ch, at : at + TIME, zh * LANES : (zh + 1) * LANES] = half

    i = lax.broadcasted_iota(jnp.int32, (256, 256), 0)
    j = lax.broadcasted_iota(jnp.int32, (256, 256), 1)
    order = jnp.where(i == (j % 32) * 8 + j // 32, 1.0, 0.0).astype(BF)
    for ch in range(4):
        cols = a_ref[ch]
        left = dot(cols, order, (1, 0))
        parts = []
        for h in range(2):
            re, im = left[2 * h * TIME : (2 * h + 1) * TIME], left[(2 * h + 1) * TIME : (2 * h + 2) * TIME]
            real, imag = jnp.concatenate([re, im], axis=0), jnp.concatenate([im, -re], axis=0)
            parts.append(jnp.concatenate([real, imag], axis=1).astype(BF))
        high, low = parts
        total = dot(jnp.concatenate([high, low], axis=0), jnp.concatenate([cols[: 2 * TIME]] * 2, axis=0), (0, 0))
        total = total + dot(high, cols[2 * TIME :], (0, 0))
        c_ref[...] = total * (1.0 / TIME)
        for block, (h, g) in enumerate(((0, 0), (1, 0), (1, 1))):
            rows = [c_ref[k * 32 + g * 16 : k * 32 + g * 16 + 16, h * LANES : (h + 1) * LANES] for k in range(16)]
            for s, part in enumerate(swap_chunks(rows, 8)):
                at = block * 256 + s * 16
                d_ref[at : at + 16, ch * LANES : (ch + 1) * LANES] = part.astype(BF)

    r = jnp.concatenate([tiles_ref[0:1], tiles_ref[1:2]], axis=1).astype(jnp.int32)
    s = jnp.concatenate([tiles_ref[2:3], tiles_ref[3:4]], axis=1).astype(jnp.int32)
    rh, sh = jnp.where(r >= 16, 1, 0), jnp.where(s >= 16, 1, 0)
    index = (rh + sh) * 256 + (s - 16 * sh) * 16 + (r - 16 * rh)
    pick = jnp.where(lax.broadcasted_iota(jnp.int32, (768, 256), 0) == index, 1.0, 0.0).astype(BF)
    c_ref[:256, :] = dot(pick, d_ref[:, :256], (0, 0))
    c_ref[256:, :] = dot(pick, d_ref[:, 256:], (0, 0))
    for d in range(16):
        for ch in range(4):
            at = (ch // 2) * 256 + (d // 8) * LANES + (d % 8) * SLOT
            rows = c_ref[at : at + SLOT, (ch % 2) * LANES : (ch % 2 + 1) * LANES]
            f_ref[d * 48 + ch * SLOT : d * 48 + (ch + 1) * SLOT, :] = rows
    out_ref[...] = f_ref[...].reshape(16, 48, LANES).astype(BF)


def place_kernel(in_ref, out_ref, f_ref):
    f_ref[...] = in_ref[...].astype(F32).reshape(f_ref.shape)
    for l in range(OWN):
        out_ref[l] = f_ref[pl.ds(l, 64, stride=SLOT), :]


PARAMS = pltpu.CompilerParams(vmem_limit_bytes=VMEM)


def per_device(voltages, fir_taps, tile_map):
    hbm = pl.BlockSpec(memory_space=pltpu.MemorySpace.HBM)
    arrays = (tile_map.T, voltages, fir_taps, jnp.asarray(dft_table()))
    sent = pl.pallas_call(
        tap_kernel,
        out_shape=jax.ShapeDtypeStruct((X * ZR * C, 72, LANES), BF),
        in_specs=[hbm] * 4,
        scratch_shapes=[
            pltpu.SMEM((2, OWN), jnp.int32),
            pltpu.VMEM((16, 2 * NCHAN), jnp.int32),
            pltpu.VMEM((TAPS, NCHAN), F32),
            pltpu.VMEM((256, 8 * QUARTER), BF),
            pltpu.SemaphoreType.DMA((4,)),
        ],
        compiler_params=PARAMS,
        name="taps",
    )(*(pltpu.with_memory_space_constraint(a, pltpu.MemorySpace.HBM) for a in arrays))
    came = lax.all_to_all(sent, ("x", "zr", "c"), 0, 0, tiled=True)
    sent, tiles = pl.pallas_call(
        sum_kernel,
        out_shape=(
            jax.ShapeDtypeStruct((Y, 56, LANES), BF),
            jax.ShapeDtypeStruct((8, LANES), F32),
        ),
        scratch_shapes=[pltpu.VMEM((Y * 56, LANES), F32)],
        compiler_params=PARAMS,
        name="sum",
    )(came)
    came = lax.all_to_all(sent, "y", 0, 0, tiled=True)
    sent = pl.pallas_call(
        turn_kernel,
        out_shape=jax.ShapeDtypeStruct((ZH * ZQ, FRAMES * X * Y, LANES), BF),
        scratch_shapes=[pltpu.VMEM((Y * 56, LANES), F32)],
        compiler_params=PARAMS,
        name="turn",
    )(came)
    came = lax.all_to_all(sent, ("zh", "zq"), 0, 0, tiled=True)
    sent = pl.pallas_call(
        correlate_kernel,
        out_shape=jax.ShapeDtypeStruct((16, 4 * SLOT, LANES), BF),
        scratch_shapes=[
            pltpu.VMEM((768, LANES), F32),
            pltpu.VMEM((4, 4 * TIME, 256), BF),
            pltpu.VMEM((512, 256), F32),
            pltpu.VMEM((768, 512), BF),
        ],
        compiler_params=PARAMS,
        name="correlate",
    )(came, tiles)
    came = lax.all_to_all(sent, ("x", "zr", "c"), 0, 0, tiled=True)
    return pl.pallas_call(
        place_kernel,
        out_shape=jax.ShapeDtypeStruct((OWN, 64, LANES), F32),
        scratch_shapes=[pltpu.VMEM((16 * 4 * SLOT, LANES), F32)],
        compiler_params=PARAMS,
        name="place",
    )(came)


def solution(mesh):
    fine = Mesh(mesh.devices.reshape(ZH, Y, X, ZQ, ZR, C), ("zh", "y") + TILE_AXES)
    in_specs = (P(TILE_AXES, ("zh", "y"), None), P(), P(TILE_AXES, None))
    out_specs = P(TILE_AXES, ("zh", "y"), None)
    return jax.shard_map(per_device, mesh=fine, in_specs=in_specs, out_specs=out_specs, check_vma=False)
```

```python
import math

import jax
import jax.numpy as jnp
import ml_dtypes
import numpy as np
from jax import lax
from jax.experimental import pallas as pl
from jax.experimental.pallas import tpu as pltpu
from jax.sharding import Mesh, PartitionSpec as P

NCHAN = 1024
QUARTER = NCHAN // 4
TIME = 48
TAPS = 4
FRAMES = 4 + TAPS - 1
LANES = 128
ZH, Y, X, ZQ, ZR, C = 2, 8, 4, 3, 2, 2
TILE_AXES = ("x", "zq", "zr", "c")
OWN = 11
SLOT = 12
VMEM = 48 * 1024 * 1024

BF = jnp.bfloat16
F32 = jnp.float32


def dft_table():
    x, zr, c, zh, y = np.meshgrid(*(np.arange(n) for n in (X, ZR, C, ZH, Y)), indexing="ij")
    first = ((zh * Y + y) * 64 + ((x * ZR + zr) * C + c) * 4).reshape(-1)
    channels = first[:, None] + np.arange(4)[None, :]
    products = channels[:, :, None] * np.arange(QUARTER)[None, None, :] % NCHAN
    angles = products.astype(np.float32) * np.float32(2.0 * math.pi / NCHAN)
    scale = np.float32(1.0 / math.sqrt(NCHAN))
    both = np.stack([np.cos(angles) * scale, np.sin(angles) * scale], axis=2)
    return both.reshape(256, 8 * QUARTER).astype(ml_dtypes.bfloat16)


def swap_chunks(rows, width):
    rows = list(rows)
    chunk = lax.broadcasted_iota(jnp.int32, rows[0].shape, 1) // width
    step = len(rows) // 2
    while step:
        low = (chunk & step) == 0
        for g in range(len(rows)):
            if not g & step:
                a, b = rows[g], rows[g + step]
                rows[g] = jnp.where(low, a, pltpu.roll(b, step * width, 1))
                rows[g + step] = jnp.where(low, pltpu.roll(a, LANES - step * width, 1), b)
        step //= 2
    return rows


def dot(a, b, contract):
    return lax.dot_general(a, b, ((contract[:1], contract[1:]), ((), ())), preferred_element_type=F32)


def split(value):
    high = value.astype(BF)
    return high, (value - high.astype(F32)).astype(BF)


def tap_kernel(map_hbm, volts_hbm, fir_hbm, table_hbm, out_ref, map_ref, volts_ref, fir_ref, table_ref, sems):
    pairs = ((volts_hbm.at[0], volts_ref), (fir_hbm, fir_ref), (map_hbm, map_ref), (table_hbm, table_ref))
    copies = [pltpu.make_async_copy(src, dst, sems.at[i]) for i, (src, dst) in enumerate(pairs)]
    for copy in copies:
        copy.start()
    copies[0].wait()
    copies[1].wait()
    lives = [[] for _ in range(4)]
    for k in range(TAPS):
        re, im = [], []
        for p, parts in enumerate((re, im)):
            for q in range(4):
                at = q * QUARTER
                part = volts_ref[:, p * NCHAN + at : p * NCHAN + at + QUARTER].astype(F32) * 0.25
                parts.append(fir_ref[k : k + 1, at : at + QUARTER] * part)
        evens = [(v[0] + v[2], v[1] + v[3]) for v in (re, im)]
        odds = [(v[0] - v[2], v[1] - v[3]) for v in (re, im)]
        sums = (
            (evens[0][0] + evens[0][1], evens[1][0] + evens[1][1]),
            (odds[0][0] + odds[1][1], odds[1][0] - odds[0][1]),
            (evens[0][0] - evens[0][1], evens[1][0] - evens[1][1]),
            (odds[0][0] - odds[1][1], odds[1][0] + odds[0][1]),
        )
        for j, (r, m) in enumerate(sums):
            lives[j] += [jnp.concatenate([r, m], axis=1), jnp.concatenate([m, -r], axis=1)]
    copies[3].wait()
    outs = []
    for j in range(4):
        table = table_ref[:, j * 2 * QUARTER : (j + 1) * 2 * QUARTER]
        high, low = split(jnp.concatenate(lives[j], axis=0))
        outs.append(dot(table, high, (1, 1)) + dot(table, low, (1, 1)))
    for k, part in enumerate(swap_chunks(outs, 32)):
        out_ref[:, k * 16 : (k + 1) * 16, :] = part.astype(BF).reshape(16, 16, LANES)

    copies[2].wait()
    sub = lax.broadcasted_iota(jnp.int32, (8, LANES), 0)
    lane = lax.broadcasted_iota(jnp.int32, (8, LANES), 1)
    own = (lax.axis_index("x") * ZR + lax.axis_index("zr")) * C + lax.axis_index("c")
    place = lane + (sub % 2) * (8 * SLOT) - own * SLOT
    tiles = jnp.zeros((8, LANES), jnp.int32)
    for l in range(OWN):
        tiles = jnp.where(place == l, jnp.where(sub < 2, map_ref[0, l], map_ref[1, l]), tiles)
    tiles = jnp.where((sub < 4) & (lane < 8 * SLOT), tiles, 0).astype(F32).astype(BF)
    for d in range(16):
        out_ref[d, 64:72, :] = tiles


def sum_kernel(in_ref, out_ref, tiles_ref, f_ref):
    for x in range(X):
        for f in range(FRAMES):
            total = None
            for k in range(TAPS):
                if 0 <= f - k < 4:
                    part = in_ref[x * 4 + f - k, k * 16 : (k + 1) * 16, :].astype(F32)
                    total = part if total is None else total + part
            f_ref[pl.ds(x * 8 + f, ZH * Y, stride=32), :] = total
        f_ref[pl.ds(x * 8 + FRAMES, ZH * Y, stride=32), :] = jnp.zeros((ZH * Y, LANES), F32)
    for zh in range(ZH):
        block = f_ref[zh * 256 : (zh + 1) * 256, :].reshape(Y, 32, LANES).astype(BF)
        for zq in range(ZQ):
            at = (zh * ZQ + zq) * Y
            out_ref[at : at + Y] = block
    tiles_ref[...] = sum(in_ref[d, 64:72, :].astype(F32) for d in range(16))


def correlate_kernel(in_ref, tiles_ref, out_ref, f_ref, a_ref, c_ref, d_ref):
    f_ref[...] = in_ref[...].astype(F32).reshape(f_ref.shape)
    upper = lax.broadcasted_iota(jnp.int32, (8, LANES), 0) < 4

    def frames(zh, y):
        at = [((zh * ZQ + q % ZQ) * Y + y) * 32 + q // ZQ * 8 for q in range(X * ZQ)]
        own = [f_ref[a : a + 8, :] for a in at]
        turned = [pltpu.roll(v, 4, 0) for v in own]
        before = [jnp.zeros((8, LANES), F32)] + turned
        return jnp.concatenate(
            [own[q] + jnp.where(upper, before[q], turned[q + 1]) for q in range(0, X * ZQ, 2)], axis=0
        )

    for zh in range(ZH):
        groups = [frames(zh, y) for y in range(Y)]
        for k, rows in enumerate(swap_chunks(groups, 16)):
            ch, p = divmod(k, 2)
            a_ref[ch, p * TIME : (p + 1) * TIME, zh * LANES : (zh + 1) * LANES] = rows.astype(BF)

    i = lax.broadcasted_iota(jnp.int32, (256, 256), 0)
    j = lax.broadcasted_iota(jnp.int32, (256, 256), 1)
    order = jnp.where(i == (j % 32) * 8 + j // 32, 1.0, 0.0).astype(BF)
    for ch in range(4):
        cols = a_ref[ch]
        left = dot(cols, order, (1, 0))
        re, im = left[:TIME], left[TIME:]
        both = jnp.concatenate([jnp.concatenate([re, im], axis=0), jnp.concatenate([im, -re], axis=0)], axis=1)
        c_ref[...] = dot(both.astype(BF), cols, (0, 0)) * (1.0 / TIME)
        for block, (h, g) in enumerate(((0, 0), (1, 0), (1, 1))):
            rows = [c_ref[k * 32 + g * 16 : k * 32 + g * 16 + 16, h * LANES : (h + 1) * LANES] for k in range(16)]
            for s, part in enumerate(swap_chunks(rows, 8)):
                at = block * 256 + s * 16
                d_ref[at : at + 16, ch * LANES : (ch + 1) * LANES] = part.astype(BF)

    r = jnp.concatenate([tiles_ref[0:1], tiles_ref[1:2]], axis=1).astype(jnp.int32)
    s = jnp.concatenate([tiles_ref[2:3], tiles_ref[3:4]], axis=1).astype(jnp.int32)
    rh, sh = jnp.where(r >= 16, 1, 0), jnp.where(s >= 16, 1, 0)
    index = (rh + sh) * 256 + (s - 16 * sh) * 16 + (r - 16 * rh)
    pick = jnp.where(lax.broadcasted_iota(jnp.int32, (768, 256), 0) == index, 1.0, 0.0).astype(BF)
    c_ref[:256, :] = dot(pick, d_ref[:, :256], (0, 0))
    c_ref[256:, :] = dot(pick, d_ref[:, 256:], (0, 0))
    for d in range(16):
        for ch in range(4):
            at = (ch // 2) * 256 + (d // 8) * LANES + (d % 8) * SLOT
            rows = c_ref[at : at + SLOT, (ch % 2) * LANES : (ch % 2 + 1) * LANES]
            f_ref[d * 48 + ch * SLOT : d * 48 + (ch + 1) * SLOT, :] = rows
    out_ref[...] = f_ref[: 16 * 48, :].reshape(16, 48, LANES).astype(BF)


def place_kernel(in_ref, out_ref, f_ref):
    f_ref[...] = in_ref[...].astype(F32).reshape(f_ref.shape)
    for l in range(OWN):
        out_ref[l] = f_ref[pl.ds(l, 64, stride=SLOT), :]


PARAMS = pltpu.CompilerParams(vmem_limit_bytes=VMEM)


def per_device(voltages, fir_taps, tile_map):
    hbm = pl.BlockSpec(memory_space=pltpu.MemorySpace.HBM)
    arrays = (tile_map.T, voltages, fir_taps, jnp.asarray(dft_table()))
    sent = pl.pallas_call(
        tap_kernel,
        out_shape=jax.ShapeDtypeStruct((X * ZR * C, 72, LANES), BF),
        in_specs=[hbm] * 4,
        scratch_shapes=[
            pltpu.SMEM((2, OWN), jnp.int32),
            pltpu.VMEM((16, 2 * NCHAN), jnp.int32),
            pltpu.VMEM((TAPS, NCHAN), F32),
            pltpu.VMEM((256, 8 * QUARTER), BF),
            pltpu.SemaphoreType.DMA((4,)),
        ],
        compiler_params=PARAMS,
        name="taps",
    )(*(pltpu.with_memory_space_constraint(a, pltpu.MemorySpace.HBM) for a in arrays))
    came = lax.all_to_all(sent, ("x", "zr", "c"), 0, 0, tiled=True)
    sent, tiles = pl.pallas_call(
        sum_kernel,
        out_shape=(
            jax.ShapeDtypeStruct((ZH * ZQ * Y, 32, LANES), BF),
            jax.ShapeDtypeStruct((8, LANES), F32),
        ),
        scratch_shapes=[pltpu.VMEM((ZH * Y * 32, LANES), F32)],
        compiler_params=PARAMS,
        name="sum",
    )(came)
    came = lax.all_to_all(sent, ("zh", "zq", "y"), 0, 0, tiled=True)
    sent = pl.pallas_call(
        correlate_kernel,
        out_shape=jax.ShapeDtypeStruct((16, 4 * SLOT, LANES), BF),
        scratch_shapes=[
            pltpu.VMEM((ZH * ZQ * Y * 32, LANES), F32),
            pltpu.VMEM((4, 2 * TIME, 256), BF),
            pltpu.VMEM((512, 256), F32),
            pltpu.VMEM((768, 512), BF),
        ],
        compiler_params=PARAMS,
        name="correlate",
    )(came, tiles)
    came = lax.all_to_all(sent, ("x", "zr", "c"), 0, 0, tiled=True)
    return pl.pallas_call(
        place_kernel,
        out_shape=jax.ShapeDtypeStruct((OWN, 64, LANES), F32),
        scratch_shapes=[pltpu.VMEM((16 * 4 * SLOT, LANES), F32)],
        compiler_params=PARAMS,
        name="place",
    )(came)


def solution(mesh):
    fine = Mesh(mesh.devices.reshape(ZH, Y, X, ZQ, ZR, C), ("zh", "y") + TILE_AXES)
    in_specs = (P(TILE_AXES, ("zh", "y"), None), P(), P(TILE_AXES, None))
    out_specs = P(TILE_AXES, ("zh", "y"), None)
    return jax.shard_map(per_device, mesh=fine, in_specs=in_specs, out_specs=out_specs, check_vma=False)
```

```python
import math

import jax
import jax.numpy as jnp
import ml_dtypes
import numpy as np
from jax import lax
from jax.experimental import pallas as pl
from jax.experimental.pallas import tpu as pltpu
from jax.sharding import Mesh, PartitionSpec as P

NCHAN = 1024
QUARTER = NCHAN // 4
TIME = 48
TAPS = 4
FRAMES = 4 + TAPS - 1
LANES = 128
ZH, Y, X, ZQ, ZR, C = 2, 8, 4, 3, 2, 2
TILE_AXES = ("x", "zq", "zr", "c")
OWN = 11
SLOT = 12
VMEM = 48 * 1024 * 1024

BF = jnp.bfloat16
F32 = jnp.float32


def dft_table():
    x, zr, c, zh, y = np.meshgrid(*(np.arange(n) for n in (X, ZR, C, ZH, Y)), indexing="ij")
    first = ((zh * Y + y) * 64 + ((x * ZR + zr) * C + c) * 4).reshape(-1)
    channels = first[:, None] + np.arange(4)[None, :]
    products = channels[:, :, None] * np.arange(QUARTER)[None, None, :] % NCHAN
    angles = products.astype(np.float32) * np.float32(2.0 * math.pi / NCHAN)
    scale = np.float32(1.0 / math.sqrt(NCHAN))
    both = np.stack([np.cos(angles) * scale, np.sin(angles) * scale], axis=2)
    return both.reshape(256, 8 * QUARTER).astype(ml_dtypes.bfloat16)


def swap_chunks(rows, width):
    rows = list(rows)
    chunk = lax.broadcasted_iota(jnp.int32, rows[0].shape, 1) // width
    step = len(rows) // 2
    while step:
        low = (chunk & step) == 0
        for g in range(len(rows)):
            if not g & step:
                a, b = rows[g], rows[g + step]
                rows[g] = jnp.where(low, a, pltpu.roll(b, step * width, 1))
                rows[g + step] = jnp.where(low, pltpu.roll(a, LANES - step * width, 1), b)
        step //= 2
    return rows


def dot(a, b, contract):
    return lax.dot_general(a, b, ((contract[:1], contract[1:]), ((), ())), preferred_element_type=F32)


def split(value):
    high = value.astype(BF)
    return high, (value - high.astype(F32)).astype(BF)


def tap_kernel(map_hbm, volts_hbm, fir_hbm, table_hbm, out_ref, map_ref, volts_ref, fir_ref, table_ref, sems):
    pairs = ((volts_hbm.at[0], volts_ref), (fir_hbm, fir_ref), (map_hbm, map_ref), (table_hbm, table_ref))
    copies = [pltpu.make_async_copy(src, dst, sems.at[i]) for i, (src, dst) in enumerate(pairs)]
    for copy in copies:
        copy.start()
    copies[0].wait()
    copies[1].wait()
    lives = [[] for _ in range(4)]
    for k in range(TAPS):
        re, im = [], []
        for p, parts in enumerate((re, im)):
            for q in range(4):
                at = q * QUARTER
                part = volts_ref[:, p * NCHAN + at : p * NCHAN + at + QUARTER].astype(F32) * 0.25
                parts.append(fir_ref[k : k + 1, at : at + QUARTER] * part)
        evens = [(v[0] + v[2], v[1] + v[3]) for v in (re, im)]
        odds = [(v[0] - v[2], v[1] - v[3]) for v in (re, im)]
        sums = (
            (evens[0][0] + evens[0][1], evens[1][0] + evens[1][1]),
            (odds[0][0] + odds[1][1], odds[1][0] - odds[0][1]),
            (evens[0][0] - evens[0][1], evens[1][0] - evens[1][1]),
            (odds[0][0] - odds[1][1], odds[1][0] + odds[0][1]),
        )
        for j, (r, m) in enumerate(sums):
            lives[j] += [jnp.concatenate([r, m], axis=1), jnp.concatenate([m, -r], axis=1)]
    copies[3].wait()
    outs = []
    for j in range(4):
        table = table_ref[:, j * 2 * QUARTER : (j + 1) * 2 * QUARTER]
        high, low = split(jnp.concatenate(lives[j], axis=0))
        outs.append(dot(table, high, (1, 1)) + dot(table, low, (1, 1)))
    for k, part in enumerate(swap_chunks(outs, 32)):
        out_ref[:, k * 16 : (k + 1) * 16, :] = part.astype(BF).reshape(16, 16, LANES)

    copies[2].wait()
    sub = lax.broadcasted_iota(jnp.int32, (8, LANES), 0)
    lane = lax.broadcasted_iota(jnp.int32, (8, LANES), 1)
    own = (lax.axis_index("x") * ZR + lax.axis_index("zr")) * C + lax.axis_index("c")
    place = lane + (sub % 2) * (8 * SLOT) - own * SLOT
    tiles = jnp.zeros((8, LANES), jnp.int32)
    for l in range(OWN):
        tiles = jnp.where(place == l, jnp.where(sub < 2, map_ref[0, l], map_ref[1, l]), tiles)
    tiles = jnp.where((sub < 4) & (lane < 8 * SLOT), tiles, 0).astype(F32).astype(BF)
    for d in range(16):
        out_ref[d, 64:72, :] = tiles


def sum_kernel(in_ref, out_ref, tiles_ref, f_ref):
    for x in range(X):
        for f in range(FRAMES):
            total = None
            for k in range(TAPS):
                if 0 <= f - k < 4:
                    part = in_ref[x * 4 + f - k, k * 16 : (k + 1) * 16, :].astype(F32)
                    total = part if total is None else total + part
            f_ref[pl.ds(x * 8 + f, ZH * Y, stride=32), :] = total
        f_ref[pl.ds(x * 8 + FRAMES, ZH * Y, stride=32), :] = jnp.zeros((ZH * Y, LANES), F32)
    for zh in range(ZH):
        block = f_ref[zh * 256 : (zh + 1) * 256, :].reshape(Y, 32, LANES).astype(BF)
        for zq in range(ZQ):
            out_ref[:, zq * ZH + zh] = block
    tiles_ref[...] = sum(in_ref[d, 64:72, :].astype(F32) for d in range(16))


def correlate_kernel(in_ref, tiles_ref, out_ref, f_ref, a_ref, c_ref, d_ref):
    f_ref[...] = in_ref[...].astype(F32).reshape(f_ref.shape)
    upper = lax.broadcasted_iota(jnp.int32, (8, LANES), 0) < 4

    def frames(zh, y):
        at = [((y * ZQ + q % ZQ) * ZH + zh) * 32 + q // ZQ * 8 for q in range(X * ZQ)]
        own = [f_ref[a : a + 8, :] for a in at]
        turned = [pltpu.roll(v, 4, 0) for v in own]
        before = [jnp.zeros((8, LANES), F32)] + turned
        return jnp.concatenate(
            [own[q] + jnp.where(upper, before[q], turned[q + 1]) for q in range(0, X * ZQ, 2)], axis=0
        )

    for zh in range(ZH):
        groups = [frames(zh, y) for y in range(Y)]
        for k, rows in enumerate(swap_chunks(groups, 16)):
            ch, p = divmod(k, 2)
            a_ref[ch, p * TIME : (p + 1) * TIME, zh * LANES : (zh + 1) * LANES] = rows.astype(BF)

    i = lax.broadcasted_iota(jnp.int32, (256, 256), 0)
    j = lax.broadcasted_iota(jnp.int32, (256, 256), 1)
    order = jnp.where(i == (j % 32) * 8 + j // 32, 1.0, 0.0).astype(BF)
    for ch in range(4):
        cols = a_ref[ch]
        left = dot(cols, order, (1, 0))
        re, im = left[:TIME], left[TIME:]
        both = jnp.concatenate([jnp.concatenate([re, im], axis=0), jnp.concatenate([im, -re], axis=0)], axis=1)
        c_ref[...] = dot(both.astype(BF), cols, (0, 0)) * (1.0 / TIME)
        for block, (h, g) in enumerate(((0, 0), (1, 0), (1, 1))):
            rows = [c_ref[k * 32 + g * 16 : k * 32 + g * 16 + 16, h * LANES : (h + 1) * LANES] for k in range(16)]
            for s, part in enumerate(swap_chunks(rows, 8)):
                at = block * 256 + s * 16
                d_ref[at : at + 16, ch * LANES : (ch + 1) * LANES] = part.astype(BF)

    r = jnp.concatenate([tiles_ref[0:1], tiles_ref[1:2]], axis=1).astype(jnp.int32)
    s = jnp.concatenate([tiles_ref[2:3], tiles_ref[3:4]], axis=1).astype(jnp.int32)
    rh, sh = jnp.where(r >= 16, 1, 0), jnp.where(s >= 16, 1, 0)
    index = (rh + sh) * 256 + (s - 16 * sh) * 16 + (r - 16 * rh)
    pick = jnp.where(lax.broadcasted_iota(jnp.int32, (768, 256), 0) == index, 1.0, 0.0).astype(BF)
    c_ref[:256, :] = dot(pick, d_ref[:, :256], (0, 0))
    c_ref[256:, :] = dot(pick, d_ref[:, 256:], (0, 0))
    for d in range(16):
        for ch in range(4):
            at = (ch // 2) * 256 + (d // 8) * LANES + (d % 8) * SLOT
            rows = c_ref[at : at + SLOT, (ch % 2) * LANES : (ch % 2 + 1) * LANES]
            f_ref[d * 48 + ch * SLOT : d * 48 + (ch + 1) * SLOT, :] = rows
    out_ref[...] = f_ref[: 16 * 48, :].reshape(16, 48, LANES).astype(BF)


def place_kernel(in_ref, out_ref, f_ref):
    f_ref[...] = in_ref[...].astype(F32).reshape(f_ref.shape)
    for l in range(OWN):
        out_ref[l] = f_ref[pl.ds(l, 64, stride=SLOT), :]


PARAMS = pltpu.CompilerParams(vmem_limit_bytes=VMEM)


def per_device(voltages, fir_taps, tile_map):
    hbm = pl.BlockSpec(memory_space=pltpu.MemorySpace.HBM)
    arrays = (tile_map.T, voltages, fir_taps, jnp.asarray(dft_table()))
    sent = pl.pallas_call(
        tap_kernel,
        out_shape=jax.ShapeDtypeStruct((X * ZR * C, 72, LANES), BF),
        in_specs=[hbm] * 4,
        scratch_shapes=[
            pltpu.SMEM((2, OWN), jnp.int32),
            pltpu.VMEM((16, 2 * NCHAN), jnp.int32),
            pltpu.VMEM((TAPS, NCHAN), F32),
            pltpu.VMEM((256, 8 * QUARTER), BF),
            pltpu.SemaphoreType.DMA((4,)),
        ],
        compiler_params=PARAMS,
        name="taps",
    )(*(pltpu.with_memory_space_constraint(a, pltpu.MemorySpace.HBM) for a in arrays))
    came = lax.all_to_all(sent, ("x", "zr", "c"), 0, 0, tiled=True)
    sent, tiles = pl.pallas_call(
        sum_kernel,
        out_shape=(
            jax.ShapeDtypeStruct((Y, ZQ * ZH, 32, LANES), BF),
            jax.ShapeDtypeStruct((8, LANES), F32),
        ),
        scratch_shapes=[pltpu.VMEM((ZH * Y * 32, LANES), F32)],
        compiler_params=PARAMS,
        name="sum",
    )(came)
    came = lax.all_to_all(sent.reshape(Y * ZQ * ZH, 32, LANES), ("y", "zq", "zh"), 0, 0, tiled=True)
    sent = pl.pallas_call(
        correlate_kernel,
        out_shape=jax.ShapeDtypeStruct((16, 4 * SLOT, LANES), BF),
        scratch_shapes=[
            pltpu.VMEM((ZH * ZQ * Y * 32, LANES), F32),
            pltpu.VMEM((4, 2 * TIME, 256), BF),
            pltpu.VMEM((512, 256), F32),
            pltpu.VMEM((768, 512), BF),
        ],
        compiler_params=PARAMS,
        name="correlate",
    )(came, tiles)
    came = lax.all_to_all(sent, ("x", "zr", "c"), 0, 0, tiled=True)
    return pl.pallas_call(
        place_kernel,
        out_shape=jax.ShapeDtypeStruct((OWN, 64, LANES), F32),
        scratch_shapes=[pltpu.VMEM((16 * 4 * SLOT, LANES), F32)],
        compiler_params=PARAMS,
        name="place",
    )(came)


def solution(mesh):
    fine = Mesh(mesh.devices.reshape(ZH, Y, X, ZQ, ZR, C), ("zh", "y") + TILE_AXES)
    in_specs = (P(TILE_AXES, ("zh", "y"), None), P(), P(TILE_AXES, None))
    out_specs = P(TILE_AXES, ("zh", "y"), None)
    return jax.shard_map(per_device, mesh=fine, in_specs=in_specs, out_specs=out_specs, check_vma=False)
```

```python
import math

import jax
import jax.numpy as jnp
import ml_dtypes
import numpy as np
from jax import lax
from jax.experimental import pallas as pl
from jax.experimental.pallas import tpu as pltpu
from jax.sharding import Mesh, PartitionSpec as P

NCHAN = 1024
QUARTER = NCHAN // 4
TIME = 48
TAPS = 4
FRAMES = 4 + TAPS - 1
LANES = 128
ZH, YA, YB, X, ZQ, ZR, C = 2, 4, 2, 4, 3, 2, 2
Y = YA * YB
CT_AXES = ("zh", "ya", "yb")
TILE_AXES = ("x", "zq", "zr", "c")
OWN = 11
SLOT = 12
VMEM = 48 * 1024 * 1024

BF = jnp.bfloat16
F32 = jnp.float32


def dft_table():
    x, zr, c, yb, zh, ya = np.meshgrid(*(np.arange(n) for n in (X, ZR, C, YB, ZH, YA)), indexing="ij")
    first = ((zh * Y + ya * YB + yb) * 64 + ((x * ZR + zr) * C + c) * 4).reshape(-1)
    channels = first[:, None] + np.arange(4)[None, :]
    products = channels[:, :, None] * np.arange(QUARTER)[None, None, :] % NCHAN
    angles = products.astype(np.float32) * np.float32(2.0 * math.pi / NCHAN)
    scale = np.float32(1.0 / math.sqrt(NCHAN))
    both = np.stack([np.cos(angles) * scale, np.sin(angles) * scale], axis=2)
    return both.reshape(256, 8 * QUARTER).astype(ml_dtypes.bfloat16)


def swap_chunks(rows, width):
    rows = list(rows)
    chunk = lax.broadcasted_iota(jnp.int32, rows[0].shape, 1) // width
    step = len(rows) // 2
    while step:
        low = (chunk & step) == 0
        for g in range(len(rows)):
            if not g & step:
                a, b = rows[g], rows[g + step]
                rows[g] = jnp.where(low, a, pltpu.roll(b, step * width, 1))
                rows[g + step] = jnp.where(low, pltpu.roll(a, LANES - step * width, 1), b)
        step //= 2
    return rows


def dot(a, b, contract):
    return lax.dot_general(a, b, ((contract[:1], contract[1:]), ((), ())), preferred_element_type=F32)


def split(value):
    high = value.astype(BF)
    return high, (value - high.astype(F32)).astype(BF)


def tap_kernel(map_hbm, volts_hbm, fir_hbm, table_hbm, out_ref, map_ref, volts_ref, fir_ref, table_ref, sems):
    pairs = ((volts_hbm.at[0], volts_ref), (fir_hbm, fir_ref), (map_hbm, map_ref), (table_hbm, table_ref))
    copies = [pltpu.make_async_copy(src, dst, sems.at[i]) for i, (src, dst) in enumerate(pairs)]
    for copy in copies:
        copy.start()
    copies[0].wait()
    copies[1].wait()
    lives = [[] for _ in range(4)]
    for k in range(TAPS):
        re, im = [], []
        for p, parts in enumerate((re, im)):
            for q in range(4):
                at = q * QUARTER
                part = volts_ref[:, p * NCHAN + at : p * NCHAN + at + QUARTER].astype(F32) * 0.25
                parts.append(fir_ref[k : k + 1, at : at + QUARTER] * part)
        evens = [(v[0] + v[2], v[1] + v[3]) for v in (re, im)]
        odds = [(v[0] - v[2], v[1] - v[3]) for v in (re, im)]
        sums = (
            (evens[0][0] + evens[0][1], evens[1][0] + evens[1][1]),
            (odds[0][0] + odds[1][1], odds[1][0] - odds[0][1]),
            (evens[0][0] - evens[0][1], evens[1][0] - evens[1][1]),
            (odds[0][0] - odds[1][1], odds[1][0] + odds[0][1]),
        )
        for j, (r, m) in enumerate(sums):
            lives[j] += [jnp.concatenate([r, m], axis=1), jnp.concatenate([m, -r], axis=1)]
    copies[3].wait()
    outs = []
    for j in range(4):
        table = table_ref[:, j * 2 * QUARTER : (j + 1) * 2 * QUARTER]
        high, low = split(jnp.concatenate(lives[j], axis=0))
        outs.append(dot(table, high, (1, 1)) + dot(table, low, (1, 1)))
    parts = [part.reshape(32, 8, LANES) for part in swap_chunks(outs, 32)]

    copies[2].wait()
    sub = lax.broadcasted_iota(jnp.int32, (8, LANES), 0)
    lane = lax.broadcasted_iota(jnp.int32, (8, LANES), 1)
    own = (lax.axis_index("x") * ZR + lax.axis_index("zr")) * C + lax.axis_index("c")
    place = lane + (sub % 2) * (8 * SLOT) - own * SLOT
    tiles = jnp.zeros((8, LANES), jnp.int32)
    for l in range(OWN):
        tiles = jnp.where(place == l, jnp.where(sub < 2, map_ref[0, l], map_ref[1, l]), tiles)
    tiles = jnp.where((sub < 4) & (lane < 8 * SLOT), tiles, 0).astype(F32)
    parts.append(jnp.broadcast_to(tiles[None], (32, 8, LANES)))
    out_ref[...] = jnp.concatenate(parts, axis=1).astype(BF)


def sum_kernel(in_ref, out_ref, tiles_ref, g_ref, f_ref):
    g_ref[...] = in_ref[...].astype(F32).reshape(g_ref.shape)
    for x in range(X):
        for yb in range(YB):
            for f in range(FRAMES):
                total = None
                for k in range(TAPS):
                    if 0 <= f - k < 4:
                        at = ((x * 4 + f - k) * YB + yb) * 40 + k * 8
                        part = g_ref[at : at + 8, :]
                        total = part if total is None else total + part
                f_ref[pl.ds(f * 8 + x * YB + yb, ZH * YA, stride=56), :] = total
    for zh in range(ZH):
        block = f_ref[zh * YA * 56 : (zh + 1) * YA * 56, :].reshape(YA, 56, LANES).astype(BF)
        for zq in range(ZQ):
            out_ref[:, zq * ZH + zh] = block
    tiles_ref[...] = sum(g_ref[d * YB * 40 + 32 : d * YB * 40 + 40, :] for d in range(16))


def correlate_kernel(in_ref, tiles_ref, out_ref, f_ref, a_ref, c_ref, d_ref):
    f_ref[: 24 * 56, :] = in_ref[...].astype(F32).reshape(24 * 56, LANES)
    f_ref[24 * 56 :, :] = jnp.zeros((8, LANES), F32)
    row = lax.broadcasted_iota(jnp.int32, (8, LANES), 0)
    upper = row < 4

    def frames(zh, y):
        ya, yb = divmod(y, YB)
        at = [((ya * ZQ + q % ZQ) * ZH + zh) * 56 + q // ZQ * YB + yb for q in range(X * ZQ)]
        own = [jnp.where(row < FRAMES, f_ref[pl.ds(a, 8, stride=8), :], 0.0) for a in at]
        turned = [pltpu.roll(v, 4, 0) for v in own]
        before = [jnp.zeros((8, LANES), F32)] + turned
        return jnp.concatenate(
            [own[q] + jnp.where(upper, before[q], turned[q + 1]) for q in range(0, X * ZQ, 2)], axis=0
        )

    for zh in range(ZH):
        groups = [frames(zh, y) for y in range(Y)]
        for k, rows in enumerate(swap_chunks(groups, 16)):
            ch, p = divmod(k, 2)
            a_ref[ch, p * TIME : (p + 1) * TIME, zh * LANES : (zh + 1) * LANES] = rows.astype(BF)

    i = lax.broadcasted_iota(jnp.int32, (256, 256), 0)
    j = lax.broadcasted_iota(jnp.int32, (256, 256), 1)
    order = jnp.where(i == (j % 32) * 8 + j // 32, 1.0, 0.0).astype(BF)
    for ch in range(4):
        cols = a_ref[ch]
        left = dot(cols, order, (1, 0))
        re, im = left[:TIME], left[TIME:]
        both = jnp.concatenate([jnp.concatenate([re, im], axis=0), jnp.concatenate([im, -re], axis=0)], axis=1)
        c_ref[...] = dot(both.astype(BF), cols, (0, 0)) * (1.0 / TIME)
        for block, (h, g) in enumerate(((0, 0), (1, 0), (1, 1))):
            rows = [c_ref[k * 32 + g * 16 : k * 32 + g * 16 + 16, h * LANES : (h + 1) * LANES] for k in range(16)]
            for s, part in enumerate(swap_chunks(rows, 8)):
                at = block * 256 + s * 16
                d_ref[at : at + 16, ch * LANES : (ch + 1) * LANES] = part.astype(BF)

    r = jnp.concatenate([tiles_ref[0:1], tiles_ref[1:2]], axis=1).astype(jnp.int32)
    s = jnp.concatenate([tiles_ref[2:3], tiles_ref[3:4]], axis=1).astype(jnp.int32)
    rh, sh = jnp.where(r >= 16, 1, 0), jnp.where(s >= 16, 1, 0)
    index = (rh + sh) * 256 + (s - 16 * sh) * 16 + (r - 16 * rh)
    pick = jnp.where(lax.broadcasted_iota(jnp.int32, (768, 256), 0) == index, 1.0, 0.0).astype(BF)
    c_ref[:256, :] = dot(pick, d_ref[:, :256], (0, 0))
    c_ref[256:, :] = dot(pick, d_ref[:, 256:], (0, 0))
    for d in range(16):
        for ch in range(4):
            at = (ch // 2) * 256 + (d // 8) * LANES + (d % 8) * SLOT
            rows = c_ref[at : at + SLOT, (ch % 2) * LANES : (ch % 2 + 1) * LANES]
            f_ref[d * 48 + ch * SLOT : d * 48 + (ch + 1) * SLOT, :] = rows
    out_ref[...] = f_ref[: 16 * 48, :].reshape(16, 48, LANES).astype(BF)


def place_kernel(in_ref, out_ref, f_ref):
    f_ref[...] = in_ref[...].astype(F32).reshape(f_ref.shape)
    for l in range(OWN):
        out_ref[l] = f_ref[pl.ds(l, 64, stride=SLOT), :]


PARAMS = pltpu.CompilerParams(vmem_limit_bytes=VMEM)


def per_device(voltages, fir_taps, tile_map):
    hbm = pl.BlockSpec(memory_space=pltpu.MemorySpace.HBM)
    arrays = (tile_map.T, voltages, fir_taps, jnp.asarray(dft_table()))
    sent = pl.pallas_call(
        tap_kernel,
        out_shape=jax.ShapeDtypeStruct((X * ZR * C * YB, 40, LANES), BF),
        in_specs=[hbm] * 4,
        scratch_shapes=[
            pltpu.SMEM((2, OWN), jnp.int32),
            pltpu.VMEM((16, 2 * NCHAN), jnp.int32),
            pltpu.VMEM((TAPS, NCHAN), F32),
            pltpu.VMEM((256, 8 * QUARTER), BF),
            pltpu.SemaphoreType.DMA((4,)),
        ],
        compiler_params=PARAMS,
        name="taps",
    )(*(pltpu.with_memory_space_constraint(a, pltpu.MemorySpace.HBM) for a in arrays))
    came = lax.all_to_all(sent, ("x", "zr", "c", "yb"), 0, 0, tiled=True)
    sent, tiles = pl.pallas_call(
        sum_kernel,
        out_shape=(
            jax.ShapeDtypeStruct((YA, ZQ * ZH, 56, LANES), BF),
            jax.ShapeDtypeStruct((8, LANES), F32),
        ),
        scratch_shapes=[pltpu.VMEM((32 * 40, LANES), F32), pltpu.VMEM((ZH * YA * 56, LANES), F32)],
        compiler_params=PARAMS,
        name="sum",
    )(came)
    came = lax.all_to_all(sent.reshape(YA * ZQ * ZH, 56, LANES), ("ya", "zq", "zh"), 0, 0, tiled=True)
    sent = pl.pallas_call(
        correlate_kernel,
        out_shape=jax.ShapeDtypeStruct((16, 4 * SLOT, LANES), BF),
        scratch_shapes=[
            pltpu.VMEM((24 * 56 + 8, LANES), F32),
            pltpu.VMEM((4, 2 * TIME, 256), BF),
            pltpu.VMEM((512, 256), F32),
            pltpu.VMEM((768, 512), BF),
        ],
        compiler_params=PARAMS,
        name="correlate",
    )(came, tiles)
    came = lax.all_to_all(sent, ("x", "zr", "c"), 0, 0, tiled=True)
    return pl.pallas_call(
        place_kernel,
        out_shape=jax.ShapeDtypeStruct((OWN, 64, LANES), F32),
        scratch_shapes=[pltpu.VMEM((16 * 4 * SLOT, LANES), F32)],
        compiler_params=PARAMS,
        name="place",
    )(came)


def solution(mesh):
    fine = Mesh(mesh.devices.reshape(ZH, YA, YB, X, ZQ, ZR, C), CT_AXES + TILE_AXES)
    in_specs = (P(TILE_AXES, CT_AXES, None), P(), P(TILE_AXES, None))
    out_specs = P(TILE_AXES, CT_AXES, None)
    return jax.shard_map(per_device, mesh=fine, in_specs=in_specs, out_specs=out_specs, check_vma=False)
```

```python
import math

import jax
import jax.numpy as jnp
import ml_dtypes
import numpy as np
from jax import lax
from jax.experimental import pallas as pl
from jax.experimental.pallas import tpu as pltpu
from jax.sharding import Mesh, PartitionSpec as P

NCHAN = 1024
QUARTER = NCHAN // 4
TIME = 48
TAPS = 4
FRAMES = 4 + TAPS - 1
LANES = 128
ZH, YA, YB, X, ZQ, ZR, C = 2, 4, 2, 4, 3, 2, 2
Y = YA * YB
CT_AXES = ("zh", "ya", "yb")
TILE_AXES = ("x", "zq", "zr", "c")
OWN = 11
SLOT = 12
VMEM = 48 * 1024 * 1024

BF = jnp.bfloat16
F32 = jnp.float32


def dft_table():
    x, zr, c, yb, zh, ya = np.meshgrid(*(np.arange(n) for n in (X, ZR, C, YB, ZH, YA)), indexing="ij")
    first = ((zh * Y + ya * YB + yb) * 64 + ((x * ZR + zr) * C + c) * 4).reshape(-1)
    channels = first[:, None] + np.arange(4)[None, :]
    products = channels[:, :, None] * np.arange(QUARTER)[None, None, :] % NCHAN
    angles = products.astype(np.float32) * np.float32(2.0 * math.pi / NCHAN)
    scale = np.float32(1.0 / math.sqrt(NCHAN))
    both = np.stack([np.cos(angles) * scale, np.sin(angles) * scale], axis=2)
    return both.transpose(1, 0, 2, 3).reshape(4, 256, 2 * QUARTER).astype(ml_dtypes.bfloat16)


def swap_chunks(rows, width):
    rows = list(rows)
    chunk = lax.broadcasted_iota(jnp.int32, rows[0].shape, 1) // width
    step = len(rows) // 2
    while step:
        low = (chunk & step) == 0
        for g in range(len(rows)):
            if not g & step:
                a, b = rows[g], rows[g + step]
                rows[g] = jnp.where(low, a, pltpu.roll(b, step * width, 1))
                rows[g + step] = jnp.where(low, pltpu.roll(a, LANES - step * width, 1), b)
        step //= 2
    return rows


def dot(a, b, contract):
    return lax.dot_general(a, b, ((contract[:1], contract[1:]), ((), ())), preferred_element_type=F32)


def split(value):
    high = value.astype(BF)
    return high, (value - high.astype(F32)).astype(BF)


def tap_kernel(map_hbm, volts_hbm, fir_hbm, table_hbm, out_ref, map_ref, volts_ref, fir_ref, table_ref, sems):
    pairs = [(volts_hbm.at[0], volts_ref), (fir_hbm, fir_ref), (map_hbm, map_ref)]
    pairs += [(table_hbm.at[j], table_ref.at[j]) for j in range(4)]
    copies = [pltpu.make_async_copy(src, dst, sems.at[i]) for i, (src, dst) in enumerate(pairs)]
    for copy in copies:
        copy.start()
    copies[0].wait()
    copies[1].wait()
    lives = [[] for _ in range(4)]
    for k in range(TAPS):
        re, im = [], []
        for p, parts in enumerate((re, im)):
            for q in range(4):
                at = q * QUARTER
                part = volts_ref[:, p * NCHAN + at : p * NCHAN + at + QUARTER].astype(F32) * 0.25
                parts.append(fir_ref[k : k + 1, at : at + QUARTER] * part)
        evens = [(v[0] + v[2], v[1] + v[3]) for v in (re, im)]
        odds = [(v[0] - v[2], v[1] - v[3]) for v in (re, im)]
        sums = (
            (evens[0][0] + evens[0][1], evens[1][0] + evens[1][1]),
            (odds[0][0] + odds[1][1], odds[1][0] - odds[0][1]),
            (evens[0][0] - evens[0][1], evens[1][0] - evens[1][1]),
            (odds[0][0] - odds[1][1], odds[1][0] + odds[0][1]),
        )
        for j, (r, m) in enumerate(sums):
            lives[j] += [jnp.concatenate([r, m], axis=1), jnp.concatenate([m, -r], axis=1)]
    outs = []
    for j in range(4):
        copies[3 + j].wait()
        table = table_ref[j]
        high, low = split(jnp.concatenate(lives[j], axis=0))
        outs.append(dot(table, high, (1, 1)) + dot(table, low, (1, 1)))
    parts = [part.reshape(32, 8, LANES) for part in swap_chunks(outs, 32)]

    copies[2].wait()
    sub = lax.broadcasted_iota(jnp.int32, (8, LANES), 0)
    lane = lax.broadcasted_iota(jnp.int32, (8, LANES), 1)
    own = (lax.axis_index("x") * ZR + lax.axis_index("zr")) * C + lax.axis_index("c")
    place = lane + (sub % 2) * (8 * SLOT) - own * SLOT
    tiles = jnp.zeros((8, LANES), jnp.int32)
    for l in range(OWN):
        tiles = jnp.where(place == l, jnp.where(sub < 2, map_ref[0, l], map_ref[1, l]), tiles)
    tiles = jnp.where((sub < 4) & (lane < 8 * SLOT), tiles, 0).astype(F32)
    parts.append(jnp.broadcast_to(tiles[None], (32, 8, LANES)))
    out_ref[...] = jnp.concatenate(parts, axis=1).astype(BF)


def sum_kernel(in_ref, out_ref, tiles_ref, g_ref, f_ref):
    g_ref[...] = in_ref[...].astype(F32).reshape(g_ref.shape)
    for x in range(X):
        for yb in range(YB):
            for f in range(FRAMES):
                total = None
                for k in range(TAPS):
                    if 0 <= f - k < 4:
                        at = ((x * 4 + f - k) * YB + yb) * 40 + k * 8
                        part = g_ref[at : at + 8, :]
                        total = part if total is None else total + part
                f_ref[pl.ds(f * 8 + x * YB + yb, ZH * YA, stride=56), :] = total
    for zh in range(ZH):
        block = f_ref[zh * YA * 56 : (zh + 1) * YA * 56, :].reshape(YA, 56, LANES).astype(BF)
        for zq in range(ZQ):
            out_ref[:, zq * ZH + zh] = block
    tiles_ref[...] = sum(g_ref[d * YB * 40 + 32 : d * YB * 40 + 40, :] for d in range(16))


def correlate_kernel(in_ref, tiles_ref, out_ref, f_ref, a_ref, c_ref, d_ref):
    f_ref[: 24 * 56, :] = in_ref[...].astype(F32).reshape(24 * 56, LANES)
    f_ref[24 * 56 :, :] = jnp.zeros((64, LANES), F32)
    row = lax.broadcasted_iota(jnp.int32, (8, LANES), 0)
    upper = row < 4

    def frames(zh, y):
        ya, yb = divmod(y, YB)
        at = [((ya * ZQ + q % ZQ) * ZH + zh) * 56 + q // ZQ * YB + yb for q in range(X * ZQ)]
        own = [jnp.where(row < FRAMES, f_ref[pl.ds(a, 8, stride=8), :], 0.0) for a in at]
        turned = [pltpu.roll(v, 4, 0) for v in own]
        before = [jnp.zeros((8, LANES), F32)] + turned
        return jnp.concatenate(
            [own[q] + jnp.where(upper, before[q], turned[q + 1]) for q in range(0, X * ZQ, 2)], axis=0
        )

    for zh in range(ZH):
        groups = [frames(zh, y) for y in range(Y)]
        for k, rows in enumerate(swap_chunks(groups, 16)):
            ch, p = divmod(k, 2)
            a_ref[ch, p * TIME : (p + 1) * TIME, zh * LANES : (zh + 1) * LANES] = rows.astype(BF)

    i = lax.broadcasted_iota(jnp.int32, (256, 256), 0)
    j = lax.broadcasted_iota(jnp.int32, (256, 256), 1)
    order = jnp.where(i == (j % 32) * 8 + j // 32, 1.0, 0.0).astype(BF)
    for ch in range(4):
        cols = a_ref[ch]
        left = dot(cols, order, (1, 0))
        re, im = left[:TIME], left[TIME:]
        both = jnp.concatenate([jnp.concatenate([re, im], axis=0), jnp.concatenate([im, -re], axis=0)], axis=1)
        c_ref[...] = dot(both.astype(BF), cols, (0, 0)) * (1.0 / TIME)
        for block, (h, g) in enumerate(((0, 0), (1, 0), (1, 1))):
            rows = [c_ref[k * 32 + g * 16 : k * 32 + g * 16 + 16, h * LANES : (h + 1) * LANES] for k in range(16)]
            for s, part in enumerate(swap_chunks(rows, 8)):
                at = block * 256 + s * 16
                d_ref[at : at + 16, ch * LANES : (ch + 1) * LANES] = part.astype(BF)

    r = jnp.concatenate([tiles_ref[0:1], tiles_ref[1:2]], axis=1).astype(jnp.int32)
    s = jnp.concatenate([tiles_ref[2:3], tiles_ref[3:4]], axis=1).astype(jnp.int32)
    rh, sh = jnp.where(r >= 16, 1, 0), jnp.where(s >= 16, 1, 0)
    index = (rh + sh) * 256 + (s - 16 * sh) * 16 + (r - 16 * rh)
    pick = jnp.where(lax.broadcasted_iota(jnp.int32, (768, 256), 0) == index, 1.0, 0.0).astype(BF)
    c_ref[:256, :] = dot(pick, d_ref[:, :256], (0, 0))
    c_ref[256:, :] = dot(pick, d_ref[:, 256:], (0, 0))
    for d in range(16):
        for ch in range(4):
            at = (ch // 2) * 256 + (d // 8) * LANES + (d % 8) * SLOT
            rows = c_ref[at : at + SLOT, (ch % 2) * LANES : (ch % 2 + 1) * LANES]
            f_ref[d * 48 + ch * SLOT : d * 48 + (ch + 1) * SLOT, :] = rows
    out_ref[...] = f_ref[: 16 * 48, :].reshape(16, 48, LANES).astype(BF)


def place_kernel(in_ref, out_ref, f_ref):
    f_ref[: 16 * 48, :] = in_ref[...].astype(F32).reshape(16 * 48, LANES)
    for l in range(OWN):
        out_ref[l] = f_ref[pl.ds(l, 64, stride=SLOT), :]


PARAMS = pltpu.CompilerParams(vmem_limit_bytes=VMEM)


def per_device(voltages, fir_taps, tile_map):
    hbm = pl.BlockSpec(memory_space=pltpu.MemorySpace.HBM)
    arrays = (tile_map.T, voltages, fir_taps, jnp.asarray(dft_table()))
    sent = pl.pallas_call(
        tap_kernel,
        out_shape=jax.ShapeDtypeStruct((X * ZR * C * YB, 40, LANES), BF),
        in_specs=[hbm] * 4,
        scratch_shapes=[
            pltpu.SMEM((2, OWN), jnp.int32),
            pltpu.VMEM((16, 2 * NCHAN), jnp.int32),
            pltpu.VMEM((TAPS, NCHAN), F32),
            pltpu.VMEM((4, 256, 2 * QUARTER), BF),
            pltpu.SemaphoreType.DMA((7,)),
        ],
        compiler_params=PARAMS,
        name="taps",
    )(*(pltpu.with_memory_space_constraint(a, pltpu.MemorySpace.HBM) for a in arrays))
    came = lax.all_to_all(sent, ("x", "zr", "c", "yb"), 0, 0, tiled=True)
    sent, tiles = pl.pallas_call(
        sum_kernel,
        out_shape=(
            jax.ShapeDtypeStruct((YA, ZQ * ZH, 56, LANES), BF),
            jax.ShapeDtypeStruct((8, LANES), F32),
        ),
        scratch_shapes=[pltpu.VMEM((32 * 40, LANES), F32), pltpu.VMEM((ZH * YA * 56 + 56, LANES), F32)],
        compiler_params=PARAMS,
        name="sum",
    )(came)
    came = lax.all_to_all(sent.reshape(YA * ZQ * ZH, 56, LANES), ("ya", "zq", "zh"), 0, 0, tiled=True)
    sent = pl.pallas_call(
        correlate_kernel,
        out_shape=jax.ShapeDtypeStruct((16, 4 * SLOT, LANES), BF),
        scratch_shapes=[
            pltpu.VMEM((24 * 56 + 64, LANES), F32),
            pltpu.VMEM((4, 2 * TIME, 256), BF),
            pltpu.VMEM((512, 256), F32),
            pltpu.VMEM((768, 512), BF),
        ],
        compiler_params=PARAMS,
        name="correlate",
    )(came, tiles)
    came = lax.all_to_all(sent, ("x", "zr", "c"), 0, 0, tiled=True)
    return pl.pallas_call(
        place_kernel,
        out_shape=jax.ShapeDtypeStruct((OWN, 64, LANES), F32),
        scratch_shapes=[pltpu.VMEM((16 * 4 * SLOT + 16, LANES), F32)],
        compiler_params=PARAMS,
        name="place",
    )(came)


def solution(mesh):
    fine = Mesh(mesh.devices.reshape(ZH, YA, YB, X, ZQ, ZR, C), CT_AXES + TILE_AXES)
    in_specs = (P(TILE_AXES, CT_AXES, None), P(), P(TILE_AXES, None))
    out_specs = P(TILE_AXES, CT_AXES, None)
    return jax.shard_map(per_device, mesh=fine, in_specs=in_specs, out_specs=out_specs, check_vma=False)
```

```python
import math

import jax
import jax.numpy as jnp
import ml_dtypes
import numpy as np
from jax import lax
from jax.experimental import pallas as pl
from jax.experimental.pallas import tpu as pltpu
from jax.sharding import Mesh, PartitionSpec as P

NCHAN = 1024
QUARTER = NCHAN // 4
TIME = 48
TAPS = 4
FRAMES = 4 + TAPS - 1
LANES = 128
ZH, YA, YB, X, ZQ, ZR, C = 2, 4, 2, 4, 3, 2, 2
Y = YA * YB
CT_AXES = ("zh", "ya", "yb")
TILE_AXES = ("x", "zq", "zr", "c")
OWN = 11
SLOT = 12
VMEM = 48 * 1024 * 1024

BF = jnp.bfloat16
F32 = jnp.float32


def dft_table():
    x, zr, c, yb, zh, ya = np.meshgrid(*(np.arange(n) for n in (X, ZR, C, YB, ZH, YA)), indexing="ij")
    first = ((zh * Y + ya * YB + yb) * 64 + ((x * ZR + zr) * C + c) * 4).reshape(-1)
    channels = first[:, None] + np.arange(4)[None, :]
    products = channels[:, :, None] * np.arange(QUARTER)[None, None, :] % NCHAN
    angles = products.astype(np.float32) * np.float32(2.0 * math.pi / NCHAN)
    scale = np.float32(1.0 / math.sqrt(NCHAN))
    both = np.stack([np.cos(angles) * scale, np.sin(angles) * scale], axis=2)
    return both.transpose(1, 0, 2, 3).reshape(4, 256, 2 * QUARTER).astype(ml_dtypes.bfloat16)


def swap_chunks(rows, width):
    rows = list(rows)
    chunk = lax.broadcasted_iota(jnp.int32, rows[0].shape, 1) // width
    step = len(rows) // 2
    while step:
        low = (chunk & step) == 0
        for g in range(len(rows)):
            if not g & step:
                a, b = rows[g], rows[g + step]
                rows[g] = jnp.where(low, a, pltpu.roll(b, step * width, 1))
                rows[g + step] = jnp.where(low, pltpu.roll(a, LANES - step * width, 1), b)
        step //= 2
    return rows


def dot(a, b, contract):
    return lax.dot_general(a, b, ((contract[:1], contract[1:]), ((), ())), preferred_element_type=F32)


def split(value):
    high = value.astype(BF)
    return high, (value - high.astype(F32)).astype(BF)


def tap_kernel(map_hbm, volts_hbm, fir_hbm, table_hbm, out_ref, map_ref, volts_ref, fir_ref, table_ref, sems):
    pairs = ((volts_hbm.at[0], volts_ref), (fir_hbm, fir_ref), (map_hbm, map_ref), (table_hbm, table_ref))
    copies = [pltpu.make_async_copy(src, dst, sems.at[i]) for i, (src, dst) in enumerate(pairs)]
    for copy in copies:
        copy.start()
    copies[0].wait()
    copies[1].wait()
    lives = [[] for _ in range(4)]
    for k in range(TAPS):
        re, im = [], []
        for p, parts in enumerate((re, im)):
            for q in range(4):
                at = q * QUARTER
                part = volts_ref[:, p * NCHAN + at : p * NCHAN + at + QUARTER].astype(F32) * 0.25
                parts.append(fir_ref[k : k + 1, at : at + QUARTER] * part)
        evens = [(v[0] + v[2], v[1] + v[3]) for v in (re, im)]
        odds = [(v[0] - v[2], v[1] - v[3]) for v in (re, im)]
        sums = (
            (evens[0][0] + evens[0][1], evens[1][0] + evens[1][1]),
            (odds[0][0] + odds[1][1], odds[1][0] - odds[0][1]),
            (evens[0][0] - evens[0][1], evens[1][0] - evens[1][1]),
            (odds[0][0] - odds[1][1], odds[1][0] + odds[0][1]),
        )
        for j, (r, m) in enumerate(sums):
            lives[j] += [jnp.concatenate([r, m], axis=1), jnp.concatenate([m, -r], axis=1)]
    copies[3].wait()
    outs = []
    for j in range(4):
        table = table_ref[j]
        high, low = split(jnp.concatenate(lives[j], axis=0))
        outs.append(dot(table, high, (1, 1)) + dot(table, low, (1, 1)))
    parts = [part.reshape(32, 8, LANES) for part in swap_chunks(outs, 32)]

    copies[2].wait()
    sub = lax.broadcasted_iota(jnp.int32, (8, LANES), 0)
    lane = lax.broadcasted_iota(jnp.int32, (8, LANES), 1)
    own = (lax.axis_index("x") * ZR + lax.axis_index("zr")) * C + lax.axis_index("c")
    place = lane + (sub % 2) * (8 * SLOT) - own * SLOT
    tiles = jnp.zeros((8, LANES), jnp.int32)
    for l in range(OWN):
        tiles = jnp.where(place == l, jnp.where(sub < 2, map_ref[0, l], map_ref[1, l]), tiles)
    tiles = jnp.where((sub < 4) & (lane < 8 * SLOT), tiles, 0).astype(F32)
    parts.append(jnp.broadcast_to(tiles[None], (32, 8, LANES)))
    out_ref[...] = jnp.concatenate(parts, axis=1).astype(BF)


def sum_kernel(in_ref, out_ref, tiles_ref, g_ref, f_ref):
    g_ref[...] = in_ref[...].astype(F32).reshape(g_ref.shape)
    for x in range(X):
        for yb in range(YB):
            for f in range(FRAMES):
                total = None
                for k in range(TAPS):
                    if 0 <= f - k < 4:
                        at = ((x * 4 + f - k) * YB + yb) * 40 + k * 8
                        part = g_ref[at : at + 8, :]
                        total = part if total is None else total + part
                f_ref[pl.ds(f * 8 + x * YB + yb, ZH * YA, stride=56), :] = total
    for zh in range(ZH):
        block = f_ref[zh * YA * 56 : (zh + 1) * YA * 56, :].reshape(YA, 56, LANES).astype(BF)
        for zq in range(ZQ):
            out_ref[:, zq * ZH + zh] = block
    tiles_ref[...] = sum(g_ref[d * YB * 40 + 32 : d * YB * 40 + 40, :] for d in range(16))


def correlate_kernel(in_ref, tiles_ref, out_ref, f_ref, a_ref, c_ref, d_ref):
    f_ref[: 24 * 56, :] = in_ref[...].astype(F32).reshape(24 * 56, LANES)
    f_ref[24 * 56 :, :] = jnp.zeros((64, LANES), F32)
    row = lax.broadcasted_iota(jnp.int32, (8, LANES), 0)
    upper = row < 4

    def frames(zh, y):
        ya, yb = divmod(y, YB)
        at = [((ya * ZQ + q % ZQ) * ZH + zh) * 56 + q // ZQ * YB + yb for q in range(X * ZQ)]
        own = [jnp.where(row < FRAMES, f_ref[pl.ds(a, 8, stride=8), :], 0.0) for a in at]
        turned = [pltpu.roll(v, 4, 0) for v in own]
        before = [jnp.zeros((8, LANES), F32)] + turned
        return jnp.concatenate(
            [own[q] + jnp.where(upper, before[q], turned[q + 1]) for q in range(0, X * ZQ, 2)], axis=0
        )

    for zh in range(ZH):
        groups = [frames(zh, y) for y in range(Y)]
        for k, rows in enumerate(swap_chunks(groups, 16)):
            ch, p = divmod(k, 2)
            a_ref[ch, p * TIME : (p + 1) * TIME, zh * LANES : (zh + 1) * LANES] = rows.astype(BF)

    i = lax.broadcasted_iota(jnp.int32, (256, 256), 0)
    j = lax.broadcasted_iota(jnp.int32, (256, 256), 1)
    order = jnp.where(i == (j % 32) * 8 + j // 32, 1.0, 0.0).astype(BF)
    for ch in range(4):
        cols = a_ref[ch]
        left = dot(cols, order, (1, 0))
        re, im = left[:TIME], left[TIME:]
        both = jnp.concatenate([jnp.concatenate([re, im], axis=0), jnp.concatenate([im, -re], axis=0)], axis=1)
        c_ref[...] = dot(both.astype(BF), cols, (0, 0)) * (1.0 / TIME)
        for block, (h, g) in enumerate(((0, 0), (1, 0), (1, 1))):
            rows = [c_ref[k * 32 + g * 16 : k * 32 + g * 16 + 16, h * LANES : (h + 1) * LANES] for k in range(16)]
            for s, part in enumerate(swap_chunks(rows, 8)):
                at = block * 256 + s * 16
                d_ref[at : at + 16, ch * LANES : (ch + 1) * LANES] = part.astype(BF)

    r = jnp.concatenate([tiles_ref[0:1], tiles_ref[1:2]], axis=1).astype(jnp.int32)
    s = jnp.concatenate([tiles_ref[2:3], tiles_ref[3:4]], axis=1).astype(jnp.int32)
    rh, sh = jnp.where(r >= 16, 1, 0), jnp.where(s >= 16, 1, 0)
    index = (rh + sh) * 256 + (s - 16 * sh) * 16 + (r - 16 * rh)
    pick = jnp.where(lax.broadcasted_iota(jnp.int32, (768, 256), 0) == index, 1.0, 0.0).astype(BF)
    c_ref[:256, :] = dot(pick, d_ref[:, :256], (0, 0))
    c_ref[256:, :] = dot(pick, d_ref[:, 256:], (0, 0))
    for d in range(16):
        for ch in range(4):
            at = (ch // 2) * 256 + (d // 8) * LANES + (d % 8) * SLOT
            rows = c_ref[at : at + SLOT, (ch % 2) * LANES : (ch % 2 + 1) * LANES]
            f_ref[d * 48 + ch * SLOT : d * 48 + (ch + 1) * SLOT, :] = rows
    out_ref[...] = f_ref[: 16 * 48, :].reshape(16, 48, LANES).astype(BF)


def place_kernel(in_ref, out_ref, f_ref):
    f_ref[: 16 * 48, :] = in_ref[...].astype(F32).reshape(16 * 48, LANES)
    for l in range(OWN):
        out_ref[l] = f_ref[pl.ds(l, 64, stride=SLOT), :]


PARAMS = pltpu.CompilerParams(vmem_limit_bytes=VMEM)


def per_device(voltages, fir_taps, tile_map):
    hbm = pl.BlockSpec(memory_space=pltpu.MemorySpace.HBM)
    arrays = (tile_map.T, voltages, fir_taps, jnp.asarray(dft_table()))
    sent = pl.pallas_call(
        tap_kernel,
        out_shape=jax.ShapeDtypeStruct((X * ZR * C * YB, 40, LANES), BF),
        in_specs=[hbm] * 4,
        scratch_shapes=[
            pltpu.SMEM((2, OWN), jnp.int32),
            pltpu.VMEM((16, 2 * NCHAN), jnp.int32),
            pltpu.VMEM((TAPS, NCHAN), F32),
            pltpu.VMEM((4, 256, 2 * QUARTER), BF),
            pltpu.SemaphoreType.DMA((4,)),
        ],
        compiler_params=PARAMS,
        name="taps",
    )(*(pltpu.with_memory_space_constraint(a, pltpu.MemorySpace.HBM) for a in arrays))
    came = lax.all_to_all(sent, ("x", "zr", "c", "yb"), 0, 0, tiled=True)
    sent, tiles = pl.pallas_call(
        sum_kernel,
        out_shape=(
            jax.ShapeDtypeStruct((YA, ZQ * ZH, 56, LANES), BF),
            jax.ShapeDtypeStruct((8, LANES), F32),
        ),
        scratch_shapes=[pltpu.VMEM((32 * 40, LANES), F32), pltpu.VMEM((ZH * YA * 56 + 56, LANES), F32)],
        compiler_params=PARAMS,
        name="sum",
    )(came)
    came = lax.all_to_all(sent.reshape(YA * ZQ * ZH, 56, LANES), ("ya", "zq", "zh"), 0, 0, tiled=True)
    sent = pl.pallas_call(
        correlate_kernel,
        out_shape=jax.ShapeDtypeStruct((16, 4 * SLOT, LANES), BF),
        scratch_shapes=[
            pltpu.VMEM((24 * 56 + 64, LANES), F32),
            pltpu.VMEM((4, 2 * TIME, 256), BF),
            pltpu.VMEM((512, 256), F32),
            pltpu.VMEM((768, 512), BF),
        ],
        compiler_params=PARAMS,
        name="correlate",
    )(came, tiles)
    came = lax.all_to_all(sent, ("x", "zr", "c"), 0, 0, tiled=True)
    return pl.pallas_call(
        place_kernel,
        out_shape=jax.ShapeDtypeStruct((OWN, 64, LANES), F32),
        scratch_shapes=[pltpu.VMEM((16 * 4 * SLOT + 16, LANES), F32)],
        compiler_params=PARAMS,
        name="place",
    )(came)


def solution(mesh):
    fine = Mesh(mesh.devices.reshape(ZH, YA, YB, X, ZQ, ZR, C), CT_AXES + TILE_AXES)
    in_specs = (P(TILE_AXES, CT_AXES, None), P(), P(TILE_AXES, None))
    out_specs = P(TILE_AXES, CT_AXES, None)
    return jax.shard_map(per_device, mesh=fine, in_specs=in_specs, out_specs=out_specs, check_vma=False)
```
